256 devices in a mesh: dp: 8 (over z_hi, core), expert: 32 (over z_lo, y, x).
Axes of the slice: x: 4, y: 4, z: 8 (z_hi: 4, z_lo: 2; z = z_hi * 2 + z_lo), core: 2. Of those that a mesh axis runs over, the one named last changes fastest.
Arguments:
- tokens: bfloat16 [32768, 1152], P(('dp', 'expert')), may hold values from -6 to 6
- out_grad: bfloat16 [32768, 1152], P(('dp', 'expert')), may hold values from -6 to 6
- gates: float32 [32768, 2], P(('dp', 'expert')), may hold values from 0.05 to 1
- expert_ids: int32 [32768, 2], P(('dp', 'expert')), may hold values from 0 to 31, all different within a row; in each aligned block of 128 rows (0 to 127, 128 to 255, ...) at most 12 rows name the same one
- swap_list: int32 [32], replicated, may hold values from 0 to 31, as said below
- w_in: bfloat16 [32, 1152, 3072], P('expert', None, 'dp'), may hold values from -0.1875 to 0.1875
- w_out: bfloat16 [32, 3072, 1152], P('expert', 'dp'), may hold values from -0.109375 to 0.109375
- first_moment: float32 [32, 1152, 3072], P('expert', None, 'dp'), may hold values from -12 to 12
- second_moment: float32 [32, 1152, 3072], P('expert', None, 'dp'), may hold values from 1 to 100
Outputs:
- x_grad: bfloat16 [32768, 1152], P(('dp', 'expert'))
- adam_out: bfloat16 [32, 1152, 3072], P('expert', None, 'dp')
The draws below stay inside these ranges and needn't reach their ends.
Inputs may be any that keep to these rules, and one draw needn't show every extreme that they name: `expert_ids`: among the 128 tokens of one device no expert is named by more than 12 rows; a token's two experts differ. swap_list[e] is e or e XOR 32/2, and swap_list[swap_list[e]] = e; swap_list[0] = 16 and swap_list[31] = 15.
All inputs are finite; a program needn't handle non-finite values.
Results may differ from the reference program's by a relative error of at most 0.015.
Values may be sent and summed in bfloat16 or wider, within the bound.
A program may use at most 128 MiB of HBM per device.

```python
import math
import jax
import jax.numpy as jnp
import numpy as np
from jax import lax

D = 1152
FF = 3072
TOK_DEV = 128
ADAM_STEP = 100
EXPERTS = 32
CAP = 12
TOKENS = 32768
N_DP = 8
N_EXPERT = 32


def draw_swap_list(key, part):
    half_count = EXPERTS // 2
    flags = jax.random.randint(key, (half_count,), 0, 2).astype(jnp.int32)
    first_half = jnp.arange(half_count, dtype=jnp.int32)
    forced = jnp.logical_or(first_half == 0, first_half == half_count - 1)
    flags = jnp.where(forced, jnp.ones_like(flags), flags).astype(jnp.int32)
    low_part = first_half + flags * half_count
    high_part = first_half + half_count - flags * half_count
    return jnp.concatenate([low_part, high_part]).astype(jnp.int32)


def steps_of(stream_key, dims, pieces, smallest, top_value):
    level, own = 1.0, jax.random.fold_in(stream_key, 6)
    for axis_at, blocks in pieces:
        heights = jnp.exp(jax.random.uniform(jax.random.fold_in(own, axis_at), (blocks,), jnp.float32, smallest / len(pieces), top_value / len(pieces)))
        level = level * jnp.repeat(heights, dims[axis_at] // blocks).reshape([-1 if axis == axis_at else 1 for axis in range(len(dims))])
    return level


def deal_out(stream_key, own, number, rows, number_of, top, most, slope):
    ranking = jax.random.permutation(stream_key, number_of)
    packed, ordinary = portions_of(number_of, rows * top, most, slope, True), portions_of(number_of, rows * top, most, slope, False)
    places = jnp.arange(number_of)

    def named(lengths, offset_by):
        used = int((lengths > 0).sum())
        fixed = max(1, used // 4)
        passed = fixed + (places - fixed + offset_by * (used - fixed)) % max(1, number_of - fixed)
        return jnp.zeros((number_of,), jnp.int32).at[ranking[jnp.where(places < fixed, places, passed)]].set(jnp.asarray(lengths, jnp.int32))

    lengths = jnp.where(number % 4 == 0, named(packed, number // 4), named(ordinary, number - number // 4 - 1))
    mixed = jax.random.permutation(jax.random.fold_in(own, 3), number_of)
    giver, taker = mixed[0:number_of // 2 * 2:2], mixed[1:number_of // 2 * 2:2]
    slack = jnp.minimum(lengths[giver] - 1, most - lengths[taker]) // 2
    slack = jnp.where((giver == ranking[0]) | (taker == ranking[0]) | (lengths[taker] == 0), 0, jnp.maximum(slack, 0))
    passed = jax.random.randint(jax.random.fold_in(own, 4), (number_of // 2,), 0, 1 << 20) % (slack + 1)
    lengths = lengths.at[giver].add(-passed).at[taker].add(passed)
    items = jnp.searchsorted(jnp.cumsum(lengths), jnp.arange(rows * top), side="right").astype(jnp.int32)
    grid = items.reshape(top, rows).T
    grid = grid[jax.random.permutation(jax.random.fold_in(own, 1), rows)]
    offset_by = jax.random.randint(jax.random.fold_in(own, 2), (rows, 1), 0, top)
    return jnp.take_along_axis(grid, (jnp.arange(top)[None, :] + offset_by) % top, axis=1)


def portions_of(amount, total, bound, skew, full):
    portions = [(1 << 20) // math.isqrt(standing ** skew) + 1 for standing in range(1, amount + 1)]
    largest = bound if full else min(bound, max(-(-total // amount), total * portions[0] // sum(portions)))
    least = 1 if total - largest >= amount - 1 else 0
    holding, surplus = [largest] + [least] * (amount - 1), total - largest - least * (amount - 1)
    while surplus > 0:
        movable = [i for i in range(1, amount) if holding[i] < largest] or [i for i in range(1, amount) if holding[i] < bound]
        mass, budget = sum([portions[i] for i in movable]), surplus
        for i in movable:
            addition = min(bound - holding[i], max(1, budget * portions[i] // mass), surplus)
            holding[i] = holding[i] + addition
            surplus = surplus - addition
    return np.array(holding)


def centred(own_key, extent, deviation, reach, pieces=(), held_as=jnp.bfloat16):
    result = jax.random.normal(own_key, extent, jnp.float32) * deviation
    if len(pieces) > 0:
        result = steps_of(own_key, extent, pieces, -0.22, 0.18) * result
    return jnp.clip(result, min=-reach, max=reach).astype(held_as)


def setup_inputs(seed: int = 0) -> dict:
    key_list = jax.random.split(jax.random.key(seed), 10)
    tokens = centred(key_list[0], (TOKENS, D), 1.0, 6.0, ((0, 256),))
    out_grad = centred(key_list[1], (TOKENS, D), 1.0, 6.0, ((0, 256),))
    gates = jnp.clip(0.05 + 0.95 * jax.random.uniform(key_list[2], (TOKENS, 2), jnp.float32) ** steps_of(key_list[2], (TOKENS, 2), ((0, 256),), -0.2, 0.2), 0.05, 1.0)
    expert_ids_keys = jax.random.split(jax.random.fold_in(key_list[3], 1), TOKENS // TOK_DEV)
    expert_ids_turns = jax.random.permutation(jax.random.fold_in(key_list[3], 3), TOKENS // TOK_DEV)
    expert_ids = jax.vmap(lambda own, number: deal_out(jax.random.fold_in(key_list[3], 2), own, number, TOK_DEV, EXPERTS, 2, CAP, 1))(expert_ids_keys, expert_ids_turns).reshape((TOKENS, 2))
    swap_list = draw_swap_list(jax.random.fold_in(key_list[9], 71), 0)
    w_in = centred(key_list[5], (EXPERTS, D, FF), D ** -0.5, 0.1875, ((0, 32), (2, 8)))
    w_out = centred(key_list[6], (EXPERTS, FF, D), FF ** -0.5, 0.109375, ((0, 32), (1, 8)))
    first_moment = centred(key_list[7], (EXPERTS, D, FF), 2.0, 12.0, ((0, 32), (2, 8)), jnp.float32)
    second_moment = jnp.clip(jnp.exp(math.log(100.0) - 4.6051702 * jax.random.uniform(key_list[8], (EXPERTS, D, FF), jnp.float32) ** steps_of(key_list[8], (EXPERTS, D, FF), ((0, 32), (2, 8)), -0.2, 0.2)), 1.0, 100.0)
    return {"tokens": tokens, "out_grad": out_grad, "gates": gates, "expert_ids": expert_ids, "swap_list": swap_list, "w_in": w_in, "w_out": w_out, "first_moment": first_moment, "second_moment": second_moment}


coef_c = 0.7978845608028654
coef_a = 0.044715
beta_one = 0.9
beta_two = 0.999
adam_eps = 1e-08

def gelu_slope(pre_act):
    inner_arg = coef_c * (pre_act + coef_a * pre_act * pre_act * pre_act)
    tanh_val = jnp.tanh(inner_arg)
    return 0.5 * (1.0 + tanh_val) + 0.5 * pre_act * (1.0 - tanh_val * tanh_val) * coef_c * (1.0 + 3.0 * coef_a * pre_act * pre_act)

def reference(tokens, out_grad, gates, expert_ids, swap_list, w_in, w_out, first_moment, second_moment):
    assigned = TOKENS * 2
    flat_ids = expert_ids.reshape(-1)
    grad_pair = (gates[:, :, None] * out_grad[:, None, :].astype(jnp.float32)).astype(jnp.bfloat16).reshape(assigned, D)
    rows_most = N_DP * N_EXPERT * CAP
    group_size = FF // N_DP

    def one_expert(expert):
        hits = flat_ids == expert
        hit_count = jnp.sum(hits.astype(jnp.int32))
        picks = jnp.nonzero(hits, size=rows_most, fill_value=0)[0].astype(jnp.int32)
        valid = jnp.arange(rows_most, dtype=jnp.int32) < hit_count
        x_rows = jnp.where(valid[:, None], jnp.take(tokens, picks // 2, axis=0), jnp.zeros((), jnp.bfloat16)).astype(jnp.bfloat16)
        g_rows = jnp.where(valid[:, None], jnp.take(grad_pair, picks, axis=0), jnp.zeros((), jnp.bfloat16)).astype(jnp.bfloat16)
        w_in_e = lax.dynamic_index_in_dim(w_in, expert, 0, keepdims=False)
        w_out_e = lax.dynamic_index_in_dim(w_out, expert, 0, keepdims=False)
        pre_act = jnp.dot(x_rows, w_in_e, preferred_element_type=jnp.float32)
        act_grad = jnp.dot(g_rows, w_out_e.T, preferred_element_type=jnp.float32)
        pre_grad = (act_grad * gelu_slope(pre_act)).astype(jnp.bfloat16)
        parts = jnp.einsum('rgf,dgf->rgd', pre_grad.reshape(rows_most, N_DP, group_size).astype(jnp.float32), w_in_e.reshape(D, N_DP, group_size).astype(jnp.float32)).astype(jnp.bfloat16)
        row_grad = lax.optimization_barrier(jnp.sum(parts.astype(jnp.float32), axis=1)).astype(jnp.bfloat16)
        weight_grad = jnp.dot(x_rows.T, pre_grad, preferred_element_type=jnp.float32)
        return (picks, valid, row_grad, weight_grad)
    picks, valid, row_grads, weight_grads = lax.map(one_expert, jnp.arange(EXPERTS, dtype=jnp.int32))
    row_values = jnp.where(valid.reshape(-1)[:, None], row_grads.reshape(-1, D).astype(jnp.float32), jnp.zeros((), jnp.float32))
    grad_acc = jnp.zeros((assigned, D), jnp.float32).at[picks.reshape(-1)].add(row_values)
    x_grad = lax.optimization_barrier(jnp.sum(grad_acc.reshape(TOKENS, 2, D), axis=1)).astype(jnp.bfloat16)
    first_new = beta_one * first_moment + (1.0 - beta_one) * weight_grads
    second_new = beta_two * second_moment + (1.0 - beta_two) * weight_grads * weight_grads
    adam_full = first_new / (1.0 - beta_one ** ADAM_STEP) / (jnp.sqrt(second_new / (1.0 - beta_two ** ADAM_STEP)) + adam_eps)
    adam_full = adam_full.astype(jnp.bfloat16)
    return (x_grad, jnp.take(adam_full, swap_list.astype(jnp.int32), axis=0))
```

```python
import jax
import jax.numpy as jnp
from jax import lax
from jax.experimental import pallas as pl
from jax.experimental.pallas import tpu as pltpu
from jax.sharding import PartitionSpec as P

ADAM_STEP = 100
coef_c = 0.7978845608028654
coef_a = 0.044715
beta_one = 0.9
beta_two = 0.999
adam_eps = 1e-08

D = 1152
H = 384
T = 128
E = 32
CAP = 12
B = 2 * CAP
R = E * B
C = 384
MESH = pl.DeviceIdType.MESH
f32, bf16 = jnp.float32, jnp.bfloat16

INFO, XRAW, GRAW, WI, WO0, WO1, CWI, CWO, FWI, FWO0, FWO1, GC, GW, SWAP, BACK = (
    0, 1, 2, 3, 4, 5, 6, 7, 8, 9, 10, 11, 14, 17, 20,
)
N_ONE = 21
N_LOCAL = 9


def gelu_slope(u):
    h = jnp.tanh(coef_c * (u + coef_a * u * u * u))
    return 0.5 * (1.0 + h) + 0.5 * u * (1.0 - h * h) * coef_c * (
        1.0 + 3.0 * coef_a * u * u
    )


def dot(a, b):
    return jnp.dot(a, b, preferred_element_type=f32)


def dot_t(a, b):
    return lax.dot_general(a, b, (((1,), (1,)), ((), ())), preferred_element_type=f32)


def kernel(
    tok, og, ids, gts, win, wout, m1, m2,
    xo, xr, ao, ar,
    info, xraw, graw, pk, pt, xpk, gpk, xrv, grv, xt, sl, wi, wo, pg, rg, rt, wg, wsc, wrc, wsw, wrw, mm1, mm2, xs,
    s1, r1, lo, sx, rx, sg, rgs, st, rts,
):
    dp, e = lax.axis_index("dp"), lax.axis_index("expert")
    zh, core = dp // 2, dp % 2
    p_row = ((zh + 1 - 2 * (zh % 2)) * 2 + core, e)
    p_wgt = ((3 - zh) * 2 + core, e)
    p_core = (zh * 2 + 1 - core, e)
    p_swap = (dp, (e + E // 2) % E)

    def one(i, src, dst, dev):
        return pltpu.make_async_remote_copy(
            src_ref=src, dst_ref=dst, send_sem=s1.at[i], recv_sem=r1.at[i], device_id=dev, device_id_type=MESH
        )

    def local(i, src, dst):
        return pltpu.make_async_copy(src, dst, lo.at[i])

    def at_block(ref, q):
        return ref.at[q]

    def rows_of(ref, i, n):
        return ref[pl.ds(i * n, n)].reshape(n * B, D)

    def put_rows(ref, i, n, value):
        ref[pl.ds(i * n, n)] = value.astype(bf16).reshape(n, B, D)

    def send(src, dst, ss, rs, d):
        q = (e + d) % E
        return pltpu.make_async_remote_copy(
            src_ref=at_block(src, q), dst_ref=at_block(dst, e), send_sem=ss.at[d], recv_sem=rs.at[d],
            device_id=(dp, q), device_id_type=MESH,
        )

    def arrival(src, dst, ss, rs, d):
        q = (e + E - d) % E
        return pltpu.make_async_remote_copy(
            src_ref=at_block(src, q), dst_ref=at_block(dst, q), send_sem=ss.at[d], recv_sem=rs.at[d],
            device_id=(dp, q), device_id_type=MESH,
        )

    def send_all(src, dst, ss, rs, own):
        own.start()

        @pl.loop(1, E)
        def _(d):
            send(src, dst, ss, rs, d).start()

    def wait_all(src, dst, ss, rs, own):
        own.wait()

        @pl.loop(1, E)
        def _(d):
            arrival(src, dst, ss, rs, d).wait_recv()

    copies = [
        local(0, tok, xraw.at[pl.ds(0, T)]),
        local(1, og, graw.at[pl.ds(0, T)]),
        local(2, win.at[0], wi.at[:, pl.ds(0, H)]),
        local(3, wout.at[0], wo.at[pl.ds(0, H)]),
        local(4, m1.at[0], mm1),
        local(5, m2.at[0], mm2),
    ]
    for c in copies:
        c.start()

    iota_r = lax.broadcasted_iota(jnp.int32, (T, T), 0)
    iota_c = lax.broadcasted_iota(jnp.int32, (T, T), 1)
    eye, before = iota_r == iota_c, iota_r < iota_c
    idr = [ids[k : k + 1, :].astype(f32) for k in range(2)]

    def to_col(row):
        return jnp.sum(jnp.where(eye, row, 0.0), axis=1, keepdims=True)

    idc = [to_col(r) for r in idr]

    def count(k, j, mask):
        same = idc[k] == idr[j]
        same = jnp.logical_and(same, mask) if mask is not None else same
        return jnp.sum(jnp.where(same, 1.0, 0.0), axis=0, keepdims=True)

    rank0 = count(0, 0, before)
    rank1 = count(0, 1, None) + count(1, 1, before)
    info[0, 0:1, :] = idr[0] * float(B) + rank0
    info[0, 1:2, :] = idr[1] * float(B) + rank1
    info[0, 2:4, :] = gts[...]
    info[0, 4:8, :] = jnp.zeros((4, T), f32)

    barrier = pltpu.get_barrier_semaphore()
    for dev in (p_row, p_wgt, p_core):
        pl.semaphore_signal(barrier, inc=1, device_id=dev, device_id_type=MESH)

    @pl.loop(1, E)
    def _(d):
        pl.semaphore_signal(barrier, inc=1, device_id=(dp, (e + d) % E), device_id_type=MESH)

    pl.semaphore_wait(barrier, E + 2)

    c_info = one(INFO, info.at[0], info.at[1], p_row)
    c_x = one(XRAW, tok, xraw.at[pl.ds(T, T)], p_row)
    c_g = one(GRAW, og, graw.at[pl.ds(T, T)], p_row)
    half = H // 2
    c_wi = one(WI, win.at[0], wi.at[:, pl.ds(2 * H, H)], p_wgt)
    c_wo = [
        one(WO0 + i, wout.at[0, pl.ds(i * half, half)], wo.at[pl.ds(2 * H + i * half, half)], p_wgt)
        for i in range(2)
    ]
    c_cwi = one(CWI, win.at[0], wi.at[:, pl.ds(H, H)], p_core)
    c_cwo = one(CWO, wout.at[0], wo.at[pl.ds(H, H)], p_core)
    early = [c_info, c_x, c_g, c_wi, *c_wo, c_cwi, c_cwo]
    for c in early:
        c.start()

    def build(src):
        code = info[src, 0:2, :] + float(CAP * src)
        row = lax.broadcasted_iota(jnp.int32, (R, T), 0).astype(f32)
        hit = jnp.logical_or(row == code[0:1, :], row == code[1:2, :])
        pk[:, src * T : (src + 1) * T] = jnp.where(hit, 1.0, 0.0).astype(bf16)
        lane = lax.broadcasted_iota(jnp.int32, (T, R), 1).astype(f32)
        hit = jnp.logical_or(lane == to_col(code[0:1, :]), lane == to_col(code[1:2, :]))
        pt[src * T : (src + 1) * T, :] = jnp.where(hit, 1.0, 0.0).astype(bf16)

    build(0)
    for c in copies[:2]:
        c.wait()
    c_info.wait_recv()
    build(1)
    tile = R // 4

    c_x.wait_recv()

    @pl.loop(0, 4)
    def _(i):
        rows = pl.ds(pl.multiple_of(i * tile, tile), tile)
        put_rows(xpk, i, E // 4, dot(pk[rows, :], xraw[...]))

    own_x = local(6, at_block(xpk, e), at_block(xrv, e))
    send_all(xpk, xrv, sx, rx, own_x)

    c_g.wait_recv()

    @pl.loop(0, 4)
    def _(i):
        rows = pl.ds(pl.multiple_of(i * tile, tile), tile)
        row = (lax.broadcasted_iota(jnp.int32, (tile, T), 0) + i * tile).astype(f32)
        gate = jnp.zeros((tile, T), f32)
        for src in range(2):
            for k in range(2):
                hit = row == info[src, k : k + 1, :] + float(CAP * src)
                gate += jnp.where(hit, info[src, 2 + k : 3 + k, :], 0.0)
        gate = jnp.sum(gate, axis=1, keepdims=True)
        put_rows(gpk, i, E // 4, dot(pk[rows, :], graw[...]) * gate)

    own_g = local(7, at_block(gpk, e), at_block(grv, e))
    send_all(gpk, grv, sg, rgs, own_g)

    big, blocks = R // 2, E // 2

    def slopes(h):
        @pl.loop(0, R // big)
        def _(i):
            rows = pl.ds(pl.multiple_of(i * big, big), big)
            cols = slice(h * 2 * H, (h + 1) * 2 * H)
            sl[rows, cols] = gelu_slope(dot(rows_of(xrv, i, blocks), wi[:, cols]))

    def grads(h):
        @pl.loop(0, R // big)
        def _(i):
            rows = pl.ds(pl.multiple_of(i * big, big), big)
            cols = slice(h * 2 * H, (h + 1) * 2 * H)
            act = dot_t(rows_of(grv, i, blocks), wo[cols, :])
            pg[rows, cols] = (act * sl[rows, cols]).astype(bf16)

    copies[2].wait()
    c_cwi.wait_recv()
    wait_all(xpk, xrv, sx, rx, own_x)
    slopes(0)
    xt[...] = rows_of(xrv, 0, E).T
    c_wi.wait_recv()
    f_wi = one(FWI, wi.at[:, pl.ds(2 * H, H)], wi.at[:, pl.ds(3 * H, H)], p_core)
    f_wi.start()
    f_wi.wait_recv()
    slopes(1)
    copies[3].wait()
    c_cwo.wait_recv()
    wait_all(gpk, grv, sg, rgs, own_g)
    grads(0)
    f_wo = [
        one(FWO0 + i, wo.at[pl.ds(2 * H + i * half, half)], wo.at[pl.ds(3 * H + i * half, half)], p_core)
        for i in range(2)
    ]
    for i in range(2):
        c_wo[i].wait_recv()
        f_wo[i].start()
    for i in range(2):
        f_wo[i].wait_recv()
    grads(1)

    @pl.loop(0, 4)
    def _(i):
        rows = pl.ds(pl.multiple_of(i * tile, tile), tile)
        put_rows(rg, i, E // 4, dot_t(pg[rows, :], wi[...]))

    own_r = local(8, at_block(rg, e), at_block(rt, e))
    send_all(rg, rt, st, rts, own_r)

    n_chunks = D // C
    c_gc = [one(GC + i, wsc.at[pl.ds(i * C, C)], wrc.at[pl.ds(i * C, C)], p_core) for i in range(n_chunks)]
    c_gw = [one(GW + i, wsw.at[pl.ds(i * C, C)], wrw.at[pl.ds(i * C, C)], p_wgt) for i in range(n_chunks)]
    c_sw = [one(SWAP + i, ao.at[pl.ds(i * C, C)], ar.at[pl.ds(i * C, C)], p_swap) for i in range(n_chunks)]

    def partial_grad(i):
        rows = slice(i * C, (i + 1) * C)
        part = dot(xt[rows, :], pg[...])
        wg[rows, 0:H] = part[:, 0:H]
        wg[rows, H : 2 * H] = part[:, 2 * H : 3 * H]
        wsc[rows, 0:H] = part[:, H : 2 * H].astype(bf16)
        wsc[rows, H : 2 * H] = part[:, 3 * H : 4 * H].astype(bf16)
        c_gc[i].start()

    def pass_on(i):
        rows = slice(i * C, (i + 1) * C)
        c_gc[i].wait_recv()
        wsw[rows, :] = (wg[rows, H : 2 * H] + wrc[rows, H : 2 * H].astype(f32)).astype(bf16)
        c_gw[i].start()

    def adam(i):
        rows = slice(i * C, (i + 1) * C)
        c_gw[i].wait_recv()
        grad = wg[rows, 0:H] + wrc[rows, 0:H].astype(f32) + wrw[rows, :].astype(f32)
        first = beta_one * mm1[rows, :] + (1.0 - beta_one) * grad
        second = beta_two * mm2[rows, :] + (1.0 - beta_two) * grad * grad
        step = (first / (1.0 - beta_one**ADAM_STEP)) / (
            jnp.sqrt(second / (1.0 - beta_two**ADAM_STEP)) + adam_eps
        )
        ao[rows, :] = step.astype(bf16)
        c_sw[i].start()

    partial_grad(0)
    for i in range(1, n_chunks):
        partial_grad(i)
        pass_on(i - 1)
    pass_on(n_chunks - 1)

    for c in copies[4:]:
        c.wait()
    for i in range(n_chunks - 1):
        adam(i)

    wait_all(rg, rt, st, rts, own_r)
    xs[...] = dot(pt[T : 2 * T, :], rows_of(rt, 0, E)).astype(bf16)
    c_back = one(BACK, xs, xr, p_row)
    c_back.start()
    xo[...] = dot(pt[0:T, :], rows_of(rt, 0, E))
    adam(n_chunks - 1)

    @pl.loop(1, E)
    def _(d):
        send(xpk, xrv, sx, rx, d).wait_send()
        send(gpk, grv, sg, rgs, d).wait_send()
        send(rg, rt, st, rts, d).wait_send()

    for c in [*early, f_wi, *f_wo, *c_gc, *c_gw]:
        c.wait_send()
    for c in [*c_sw, c_back]:
        c.wait()


def shards(tokens, out_grad, gates, expert_ids, swap_list, w_in, w_out, first_moment, second_moment):
    any_spec = pl.BlockSpec(memory_space=pl.ANY)
    vmem = pl.BlockSpec(memory_space=pltpu.VMEM)
    dma = pltpu.SemaphoreType.DMA
    xo, xr, ao, ar = pl.pallas_call(
        kernel,
        out_shape=(
            jax.ShapeDtypeStruct((T, D), f32),
            jax.ShapeDtypeStruct((T, D), bf16),
            jax.ShapeDtypeStruct((D, H), bf16),
            jax.ShapeDtypeStruct((D, H), bf16),
        ),
        in_specs=[any_spec, any_spec, vmem, vmem, any_spec, any_spec, any_spec, any_spec],
        out_specs=(vmem, any_spec, vmem, any_spec),
        scratch_shapes=[
            pltpu.VMEM((2, 8, T), f32),
            pltpu.VMEM((2 * T, D), bf16),
            pltpu.VMEM((2 * T, D), bf16),
            pltpu.VMEM((R, 2 * T), bf16),
            pltpu.VMEM((2 * T, R), bf16),
            pltpu.VMEM((E, B, D), bf16),
            pltpu.VMEM((E, B, D), bf16),
            pltpu.VMEM((E, B, D), bf16),
            pltpu.VMEM((E, B, D), bf16),
            pltpu.VMEM((D, R), bf16),
            pltpu.VMEM((R, 4 * H), f32),
            pltpu.VMEM((D, 4 * H), bf16),
            pltpu.VMEM((4 * H, D), bf16),
            pltpu.VMEM((R, 4 * H), bf16),
            pltpu.VMEM((E, B, D), bf16),
            pltpu.VMEM((E, B, D), bf16),
            pltpu.VMEM((D, 2 * H), f32),
            pltpu.VMEM((D, 2 * H), bf16),
            pltpu.VMEM((D, 2 * H), bf16),
            pltpu.VMEM((D, H), bf16),
            pltpu.VMEM((D, H), bf16),
            pltpu.VMEM((D, H), f32),
            pltpu.VMEM((D, H), f32),
            pltpu.VMEM((T, D), bf16),
            dma((N_ONE,)), dma((N_ONE,)), dma((N_LOCAL,)),
            dma((E,)), dma((E,)), dma((E,)), dma((E,)), dma((E,)), dma((E,)),
        ],
        compiler_params=pltpu.CompilerParams(
            collective_id=0, has_side_effects=True, vmem_limit_bytes=60 << 20
        ),
        name="experts",
    )(tokens, out_grad, expert_ids.T, gates.T, w_in, w_out, first_moment, second_moment)
    x_grad = (xo + xr.astype(f32)).astype(bf16)
    own = lax.axis_index("expert")
    moved = jnp.sum(jnp.where(jnp.arange(E, dtype=jnp.int32) == own, swap_list, 0)) != own
    return x_grad, jnp.where(moved, ar, ao)[None]


def solution(mesh):
    token_spec = P(("dp", "expert"), None)
    in_specs = (
        token_spec, token_spec, token_spec, token_spec, P(),
        P("expert", None, "dp"), P("expert", "dp", None), P("expert", None, "dp"), P("expert", None, "dp"),
    )
    out_specs = (token_spec, P("expert", None, "dp"))
    return jax.shard_map(shards, mesh=mesh, in_specs=in_specs, out_specs=out_specs, check_vma=False)
```

```python
import jax
import jax.numpy as jnp
from jax import lax
from jax.experimental import pallas as pl
from jax.experimental.pallas import tpu as pltpu
from jax.sharding import PartitionSpec as P

ADAM_STEP = 100
coef_c = 0.7978845608028654
coef_a = 0.044715
beta_one = 0.9
beta_two = 0.999
adam_eps = 1e-08

D = 1152
H = 384
T = 128
E = 32
CAP = 12
B = 2 * CAP
R = E * B
C = 384
MESH = pl.DeviceIdType.MESH
f32, bf16 = jnp.float32, jnp.bfloat16

INFO, XRAW, GRAW, WI, WO0, WO1, CWI, CWO, FWI, FWO0, FWO1, GC, GW, SWAP, BACK = (
    0, 1, 2, 3, 4, 5, 6, 7, 8, 9, 10, 11, 14, 17, 20,
)
N_ONE = 21
N_LOCAL = 9


def gelu_slope(u):
    h = jnp.tanh(coef_c * (u + coef_a * u * u * u))
    return 0.5 * (1.0 + h) + 0.5 * u * (1.0 - h * h) * coef_c * (
        1.0 + 3.0 * coef_a * u * u
    )


def dot(a, b):
    return jnp.dot(a, b, preferred_element_type=f32)


def dot_t(a, b):
    return lax.dot_general(a, b, (((1,), (1,)), ((), ())), preferred_element_type=f32)


def kernel(
    tok, og, ids, gts, win, wout, m1, m2,
    xo, xr, ao, ar,
    info, xraw, graw, pk, pt, xpk, gpk, xrv, grv, xt, sl, wi, wo, pg, rg, rt, wg, wsc, wrc, wsw, wrw, mm1, mm2, xs,
    s1, r1, lo, sx, rx, sg, rgs, st, rts,
):
    dp, e = lax.axis_index("dp"), lax.axis_index("expert")
    zh, core = dp // 2, dp % 2
    p_row = ((zh + 1 - 2 * (zh % 2)) * 2 + core, e)
    p_wgt = ((3 - zh) * 2 + core, e)
    p_core = (zh * 2 + 1 - core, e)
    p_swap = (dp, (e + E // 2) % E)

    def one(i, src, dst, dev):
        return pltpu.make_async_remote_copy(
            src_ref=src, dst_ref=dst, send_sem=s1.at[i], recv_sem=r1.at[i], device_id=dev, device_id_type=MESH
        )

    def local(i, src, dst):
        return pltpu.make_async_copy(src, dst, lo.at[i])

    def at_block(ref, q):
        return ref.at[q]

    def rows_of(ref, i, n):
        return ref[pl.ds(i * n, n)].reshape(n * B, D)

    def put_rows(ref, i, n, value):
        ref[pl.ds(i * n, n)] = value.astype(bf16).reshape(n, B, D)

    z_lo, y, x = e // 16, (e // 4) % 4, e % 4

    def peer(d, sign):
        a, b = (d // 2) % 4, d // 8
        to_z, to_y, to_x = d % 2, (a + b) % 4, a
        return ((z_lo + to_z) % 2) * 16 + ((y + 4 + sign * to_y) % 4) * 4 + (x + 4 + sign * to_x) % 4

    def send(src, dst, ss, rs, d):
        q = peer(d, 1)
        return pltpu.make_async_remote_copy(
            src_ref=at_block(src, q), dst_ref=at_block(dst, e), send_sem=ss.at[d], recv_sem=rs.at[d],
            device_id=(dp, q), device_id_type=MESH,
        )

    def arrival(src, dst, ss, rs, d):
        q = peer(d, -1)
        return pltpu.make_async_remote_copy(
            src_ref=at_block(src, q), dst_ref=at_block(dst, q), send_sem=ss.at[d], recv_sem=rs.at[d],
            device_id=(dp, q), device_id_type=MESH,
        )

    def send_all(src, dst, ss, rs, own):
        own.start()

        @pl.loop(1, E)
        def _(d):
            send(src, dst, ss, rs, d).start()

    def wait_all(src, dst, ss, rs, own):
        own.wait()

        @pl.loop(1, E)
        def _(d):
            arrival(src, dst, ss, rs, d).wait_recv()

    copies = [
        local(0, tok, xraw.at[pl.ds(0, T)]),
        local(1, og, graw.at[pl.ds(0, T)]),
        local(2, win.at[0], wi.at[:, pl.ds(0, H)]),
        local(3, wout.at[0], wo.at[pl.ds(0, H)]),
        local(4, m1.at[0], mm1),
        local(5, m2.at[0], mm2),
    ]
    for c in copies:
        c.start()

    iota_r = lax.broadcasted_iota(jnp.int32, (T, T), 0)
    iota_c = lax.broadcasted_iota(jnp.int32, (T, T), 1)
    eye, before = iota_r == iota_c, iota_r < iota_c
    idr = [ids[k : k + 1, :].astype(f32) for k in range(2)]

    def to_col(row):
        return jnp.sum(jnp.where(eye, row, 0.0), axis=1, keepdims=True)

    idc = [to_col(r) for r in idr]

    def count(k, j, mask):
        same = idc[k] == idr[j]
        same = jnp.logical_and(same, mask) if mask is not None else same
        return jnp.sum(jnp.where(same, 1.0, 0.0), axis=0, keepdims=True)

    rank0 = count(0, 0, before)
    rank1 = count(0, 1, None) + count(1, 1, before)
    info[0, 0:1, :] = idr[0] * float(B) + rank0
    info[0, 1:2, :] = idr[1] * float(B) + rank1
    info[0, 2:4, :] = gts[...]
    info[0, 4:8, :] = jnp.zeros((4, T), f32)

    barrier = pltpu.get_barrier_semaphore()
    for dev in (p_row, p_wgt, p_core):
        pl.semaphore_signal(barrier, inc=1, device_id=dev, device_id_type=MESH)

    @pl.loop(1, E)
    def _(d):
        pl.semaphore_signal(barrier, inc=1, device_id=(dp, (e + d) % E), device_id_type=MESH)

    pl.semaphore_wait(barrier, E + 2)

    c_info = one(INFO, info.at[0], info.at[1], p_row)
    c_x = one(XRAW, tok, xraw.at[pl.ds(T, T)], p_row)
    c_g = one(GRAW, og, graw.at[pl.ds(T, T)], p_row)
    half = H // 2
    c_wi = one(WI, win.at[0], wi.at[:, pl.ds(2 * H, H)], p_wgt)
    c_wo = [
        one(WO0 + i, wout.at[0, pl.ds(i * half, half)], wo.at[pl.ds(2 * H + i * half, half)], p_wgt)
        for i in range(2)
    ]
    c_cwi = one(CWI, win.at[0], wi.at[:, pl.ds(H, H)], p_core)
    c_cwo = one(CWO, wout.at[0], wo.at[pl.ds(H, H)], p_core)
    early = [c_info, c_x, c_g, c_wi, *c_wo, c_cwi, c_cwo]
    for c in early:
        c.start()

    def build(src):
        code = info[src, 0:2, :] + float(CAP * src)
        row = lax.broadcasted_iota(jnp.int32, (R, T), 0).astype(f32)
        hit = jnp.logical_or(row == code[0:1, :], row == code[1:2, :])
        pk[:, src * T : (src + 1) * T] = jnp.where(hit, 1.0, 0.0).astype(bf16)
        lane = lax.broadcasted_iota(jnp.int32, (T, R), 1).astype(f32)
        hit = jnp.logical_or(lane == to_col(code[0:1, :]), lane == to_col(code[1:2, :]))
        pt[src * T : (src + 1) * T, :] = jnp.where(hit, 1.0, 0.0).astype(bf16)

    build(0)
    for c in copies[:2]:
        c.wait()
    c_info.wait_recv()
    build(1)
    tile = R // 4

    c_x.wait_recv()

    @pl.loop(0, 4)
    def _(i):
        rows = pl.ds(pl.multiple_of(i * tile, tile), tile)
        put_rows(xpk, i, E // 4, dot(pk[rows, :], xraw[...]))

    own_x = local(6, at_block(xpk, e), at_block(xrv, e))
    send_all(xpk, xrv, sx, rx, own_x)

    c_g.wait_recv()

    @pl.loop(0, 4)
    def _(i):
        rows = pl.ds(pl.multiple_of(i * tile, tile), tile)
        row = (lax.broadcasted_iota(jnp.int32, (tile, T), 0) + i * tile).astype(f32)
        gate = jnp.zeros((tile, T), f32)
        for src in range(2):
            for k in range(2):
                hit = row == info[src, k : k + 1, :] + float(CAP * src)
                gate += jnp.where(hit, info[src, 2 + k : 3 + k, :], 0.0)
        gate = jnp.sum(gate, axis=1, keepdims=True)
        put_rows(gpk, i, E // 4, dot(pk[rows, :], graw[...]) * gate)

    own_g = local(7, at_block(gpk, e), at_block(grv, e))
    send_all(gpk, grv, sg, rgs, own_g)

    big, blocks = R // 2, E // 2

    def slopes(h):
        @pl.loop(0, R // big)
        def _(i):
            rows = pl.ds(pl.multiple_of(i * big, big), big)
            cols = slice(h * 2 * H, (h + 1) * 2 * H)
            sl[rows, cols] = gelu_slope(dot(rows_of(xrv, i, blocks), wi[:, cols]))

    def grads(h):
        @pl.loop(0, R // big)
        def _(i):
            rows = pl.ds(pl.multiple_of(i * big, big), big)
            cols = slice(h * 2 * H, (h + 1) * 2 * H)
            act = dot_t(rows_of(grv, i, blocks), wo[cols, :])
            pg[rows, cols] = (act * sl[rows, cols]).astype(bf16)

    copies[2].wait()
    c_cwi.wait_recv()
    wait_all(xpk, xrv, sx, rx, own_x)
    slopes(0)
    xt[...] = rows_of(xrv, 0, E).T
    c_wi.wait_recv()
    f_wi = one(FWI, wi.at[:, pl.ds(2 * H, H)], wi.at[:, pl.ds(3 * H, H)], p_core)
    f_wi.start()
    f_wi.wait_recv()
    slopes(1)
    copies[3].wait()
    c_cwo.wait_recv()
    wait_all(gpk, grv, sg, rgs, own_g)
    grads(0)
    f_wo = [
        one(FWO0 + i, wo.at[pl.ds(2 * H + i * half, half)], wo.at[pl.ds(3 * H + i * half, half)], p_core)
        for i in range(2)
    ]
    for i in range(2):
        c_wo[i].wait_recv()
        f_wo[i].start()
    for i in range(2):
        f_wo[i].wait_recv()
    grads(1)

    @pl.loop(0, 4)
    def _(i):
        rows = pl.ds(pl.multiple_of(i * tile, tile), tile)
        put_rows(rg, i, E // 4, dot_t(pg[rows, :], wi[...]))

    own_r = local(8, at_block(rg, e), at_block(rt, e))
    send_all(rg, rt, st, rts, own_r)

    n_chunks = D // C
    c_gc = [one(GC + i, wsc.at[pl.ds(i * C, C)], wrc.at[pl.ds(i * C, C)], p_core) for i in range(n_chunks)]
    c_gw = [one(GW + i, wsw.at[pl.ds(i * C, C)], wrw.at[pl.ds(i * C, C)], p_wgt) for i in range(n_chunks)]
    c_sw = [one(SWAP + i, ao.at[pl.ds(i * C, C)], ar.at[pl.ds(i * C, C)], p_swap) for i in range(n_chunks)]

    def partial_grad(i):
        rows = slice(i * C, (i + 1) * C)
        part = dot(xt[rows, :], pg[...])
        wg[rows, 0:H] = part[:, 0:H]
        wg[rows, H : 2 * H] = part[:, 2 * H : 3 * H]
        wsc[rows, 0:H] = part[:, H : 2 * H].astype(bf16)
        wsc[rows, H : 2 * H] = part[:, 3 * H : 4 * H].astype(bf16)
        c_gc[i].start()

    def pass_on(i):
        rows = slice(i * C, (i + 1) * C)
        c_gc[i].wait_recv()
        wsw[rows, :] = (wg[rows, H : 2 * H] + wrc[rows, H : 2 * H].astype(f32)).astype(bf16)
        c_gw[i].start()

    def adam(i):
        rows = slice(i * C, (i + 1) * C)
        c_gw[i].wait_recv()
        grad = wg[rows, 0:H] + wrc[rows, 0:H].astype(f32) + wrw[rows, :].astype(f32)
        first = beta_one * mm1[rows, :] + (1.0 - beta_one) * grad
        second = beta_two * mm2[rows, :] + (1.0 - beta_two) * grad * grad
        step = (first / (1.0 - beta_one**ADAM_STEP)) / (
            jnp.sqrt(second / (1.0 - beta_two**ADAM_STEP)) + adam_eps
        )
        ao[rows, :] = step.astype(bf16)
        c_sw[i].start()

    partial_grad(0)
    for i in range(1, n_chunks):
        partial_grad(i)
        pass_on(i - 1)
    pass_on(n_chunks - 1)

    for c in copies[4:]:
        c.wait()
    adam(0)
    wait_all(rg, rt, st, rts, own_r)
    xs[...] = dot(pt[T : 2 * T, :], rows_of(rt, 0, E)).astype(bf16)
    c_back = one(BACK, xs, xr, p_row)
    c_back.start()
    xo[...] = dot(pt[0:T, :], rows_of(rt, 0, E))
    for i in range(1, n_chunks):
        adam(i)

    @pl.loop(1, E)
    def _(d):
        send(xpk, xrv, sx, rx, d).wait_send()
        send(gpk, grv, sg, rgs, d).wait_send()
        send(rg, rt, st, rts, d).wait_send()

    for c in [*early, f_wi, *f_wo, *c_gc, *c_gw]:
        c.wait_send()
    for c in [*c_sw, c_back]:
        c.wait()


def shards(tokens, out_grad, gates, expert_ids, swap_list, w_in, w_out, first_moment, second_moment):
    any_spec = pl.BlockSpec(memory_space=pl.ANY)
    vmem = pl.BlockSpec(memory_space=pltpu.VMEM)
    dma = pltpu.SemaphoreType.DMA
    xo, xr, ao, ar = pl.pallas_call(
        kernel,
        out_shape=(
            jax.ShapeDtypeStruct((T, D), f32),
            jax.ShapeDtypeStruct((T, D), bf16),
            jax.ShapeDtypeStruct((D, H), bf16),
            jax.ShapeDtypeStruct((D, H), bf16),
        ),
        in_specs=[any_spec, any_spec, vmem, vmem, any_spec, any_spec, any_spec, any_spec],
        out_specs=(vmem, any_spec, vmem, any_spec),
        scratch_shapes=[
            pltpu.VMEM((2, 8, T), f32),
            pltpu.VMEM((2 * T, D), bf16),
            pltpu.VMEM((2 * T, D), bf16),
            pltpu.VMEM((R, 2 * T), bf16),
            pltpu.VMEM((2 * T, R), bf16),
            pltpu.VMEM((E, B, D), bf16),
            pltpu.VMEM((E, B, D), bf16),
            pltpu.VMEM((E, B, D), bf16),
            pltpu.VMEM((E, B, D), bf16),
            pltpu.VMEM((D, R), bf16),
            pltpu.VMEM((R, 4 * H), f32),
            pltpu.VMEM((D, 4 * H), bf16),
            pltpu.VMEM((4 * H, D), bf16),
            pltpu.VMEM((R, 4 * H), bf16),
            pltpu.VMEM((E, B, D), bf16),
            pltpu.VMEM((E, B, D), bf16),
            pltpu.VMEM((D, 2 * H), f32),
            pltpu.VMEM((D, 2 * H), bf16),
            pltpu.VMEM((D, 2 * H), bf16),
            pltpu.VMEM((D, H), bf16),
            pltpu.VMEM((D, H), bf16),
            pltpu.VMEM((D, H), f32),
            pltpu.VMEM((D, H), f32),
            pltpu.VMEM((T, D), bf16),
            dma((N_ONE,)), dma((N_ONE,)), dma((N_LOCAL,)),
            dma((E,)), dma((E,)), dma((E,)), dma((E,)), dma((E,)), dma((E,)),
        ],
        compiler_params=pltpu.CompilerParams(
            collective_id=0, has_side_effects=True, vmem_limit_bytes=60 << 20
        ),
        name="experts",
    )(tokens, out_grad, expert_ids.T, gates.T, w_in, w_out, first_moment, second_moment)
    x_grad = (xo + xr.astype(f32)).astype(bf16)
    own = lax.axis_index("expert")
    moved = jnp.sum(jnp.where(jnp.arange(E, dtype=jnp.int32) == own, swap_list, 0)) != own
    return x_grad, jnp.where(moved, ar, ao)[None]


def solution(mesh):
    token_spec = P(("dp", "expert"), None)
    in_specs = (
        token_spec, token_spec, token_spec, token_spec, P(),
        P("expert", None, "dp"), P("expert", "dp", None), P("expert", None, "dp"), P("expert", None, "dp"),
    )
    out_specs = (token_spec, P("expert", None, "dp"))
    return jax.shard_map(shards, mesh=mesh, in_specs=in_specs, out_specs=out_specs, check_vma=False)
```

```python
import jax
import jax.numpy as jnp
from jax import lax
from jax.experimental import pallas as pl
from jax.experimental.pallas import tpu as pltpu
from jax.sharding import PartitionSpec as P

ADAM_STEP = 100
coef_c = 0.7978845608028654
coef_a = 0.044715
beta_one = 0.9
beta_two = 0.999
adam_eps = 1e-08

D = 1152
H = 384
T = 128
E = 32
Q = 16
CAP = 12
B = 2 * CAP
G = Q * B
R = 2 * G
HA, HB = 256, 128
MESH = pl.DeviceIdType.MESH
f32, bf16 = jnp.float32, jnp.bfloat16

OWN, SIB, RA, RAS, RB, RBS = 0, H, 2 * H, 2 * H + HA, 2 * H + 2 * HA, 2 * H + 2 * HA + HB
N_ONE = 40
N_LOCAL = 15


def gelu_slope(u):
    h = jnp.tanh(coef_c * (u + coef_a * u * u * u))
    return 0.5 * (1.0 + h) + 0.5 * u * (1.0 - h * h) * coef_c * (
        1.0 + 3.0 * coef_a * u * u
    )


def dot(a, b):
    return jnp.dot(a, b, preferred_element_type=f32)


def dot_t(a, b):
    return lax.dot_general(a, b, (((1,), (1,)), ((), ())), preferred_element_type=f32)


def kernel(
    tok, og, ids, gts, win, wout, m1, m2,
    xp, xr, ao, ar,
    info, xraw, graw, pk, pt, xpk, gpk, xrv, grv, xt, sl, wi, wo, pg, rg, rt,
    wg, wgr, wsa, wra, wsb, wrb, wsc, wrc, za, zra, zb, zrb, mm1, mm2, zs, zr, xs, keep, an,
    s1, r1, lo, sx, rx, sg, rgs, st, rts,
):
    dp, e = lax.axis_index("dp"), lax.axis_index("expert")
    zh, core = dp // 2, dp % 2
    z_lo, y, x = e // Q, (e // 4) % 4, e % 4
    me = e % Q
    p_row = ((zh + 1 - 2 * (zh % 2)) * 2 + core, e)
    p_wgt = ((3 - zh) * 2 + core, e)
    p_core = (zh * 2 + 1 - core, e)
    p_zlo = (dp, (e + Q) % E)
    used = []
    started = []

    def one(src, dst, dev):
        used.append(None)
        i = len(used) - 1
        return pltpu.make_async_remote_copy(
            src_ref=src, dst_ref=dst, send_sem=s1.at[i], recv_sem=r1.at[i], device_id=dev, device_id_type=MESH
        )

    def go(copy):
        copy.start()
        started.append(copy)

    def local(i, src, dst):
        return pltpu.make_async_copy(src, dst, lo.at[i])

    def rows_of(ref, at, n):
        return ref[pl.ds(at, n)].reshape(n * B, D)

    def put_rows(ref, at, n, value):
        ref[pl.ds(at, n)] = value.astype(bf16).reshape(n, B, D)

    def peer(d, sign):
        a, b = d % 4, d // 4
        return ((y + 4 + sign * ((a + b) % 4)) % 4) * 4 + (x + 4 + sign * a) % 4

    def send(src, dst, ss, rs, g, d):
        q = peer(d, 1)
        return pltpu.make_async_remote_copy(
            src_ref=src.at[g * Q + q], dst_ref=dst.at[g * Q + me], send_sem=ss.at[g * Q + d],
            recv_sem=rs.at[g * Q + d], device_id=(dp, z_lo * Q + q), device_id_type=MESH,
        )

    def arrival(src, dst, ss, rs, g, d):
        q = peer(d, -1)
        return pltpu.make_async_remote_copy(
            src_ref=src.at[g * Q + q], dst_ref=dst.at[g * Q + q], send_sem=ss.at[g * Q + d],
            recv_sem=rs.at[g * Q + d], device_id=(dp, z_lo * Q + q), device_id_type=MESH,
        )

    def own_block(i, src, dst, g):
        return local(i + g, src.at[g * Q + me], dst.at[g * Q + me])

    def send_all(src, dst, ss, rs, g, i):
        own_block(i, src, dst, g).start()

        @pl.loop(1, Q)
        def _(d):
            send(src, dst, ss, rs, g, d).start()

    def wait_all(src, dst, ss, rs, g, i):
        own_block(i, src, dst, g).wait()

        @pl.loop(1, Q)
        def _(d):
            arrival(src, dst, ss, rs, g, d).wait_recv()

    copies = [
        local(0, tok, xraw.at[pl.ds(0, T)]),
        local(1, og, graw.at[pl.ds(0, T)]),
        local(2, win.at[0], wi.at[:, pl.ds(OWN, H)]),
        local(3, wout.at[0], wo.at[pl.ds(OWN, H)]),
        local(4, m1.at[0], mm1),
        local(5, m2.at[0], mm2),
    ]
    for c in copies:
        c.start()

    iota_r = lax.broadcasted_iota(jnp.int32, (T, T), 0)
    iota_c = lax.broadcasted_iota(jnp.int32, (T, T), 1)
    eye, before = iota_r == iota_c, iota_r < iota_c
    idr = [ids[k : k + 1, :].astype(f32) for k in range(2)]

    def to_col(row):
        return jnp.sum(jnp.where(eye, row, 0.0), axis=1, keepdims=True)

    idc = [to_col(r) for r in idr]

    def count(k, j, mask):
        same = idc[k] == idr[j]
        same = jnp.logical_and(same, mask) if mask is not None else same
        return jnp.sum(jnp.where(same, 1.0, 0.0), axis=0, keepdims=True)

    ranks = [count(0, 0, before), count(0, 1, None) + count(1, 1, before)]
    for k in range(2):
        high = jnp.where(idr[k] >= float(Q), 1.0, 0.0)
        info[0, k : k + 1, :] = high * 1024.0 + (idr[k] - high * Q) * float(B) + ranks[k]
    info[0, 2:4, :] = gts[...]
    info[0, 4:8, :] = jnp.zeros((4, T), f32)

    barrier = pltpu.get_barrier_semaphore()
    for dev in (p_row, p_wgt, p_core, p_zlo):
        pl.semaphore_signal(barrier, inc=1, device_id=dev, device_id_type=MESH)

    @pl.loop(1, Q)
    def _(d):
        pl.semaphore_signal(barrier, inc=1, device_id=(dp, z_lo * Q + peer(d, 1)), device_id_type=MESH)

    pl.semaphore_wait(barrier, Q + 3)

    def source(ref, s):
        return ref.at[pl.ds(s * T, T)]

    c_info = [one(info.at[0], info.at[1], p_zlo), one(info.at[0], info.at[2], p_row)]
    c_x = [one(tok, source(xraw, 1), p_zlo), one(tok, source(xraw, 2), p_row)]
    c_g = [one(og, source(graw, 1), p_zlo), one(og, source(graw, 2), p_row)]
    f_info = one(info.at[2], info.at[3], p_zlo)
    f_x = one(source(xraw, 2), source(xraw, 3), p_zlo)
    f_g = one(source(graw, 2), source(graw, 3), p_zlo)

    def columns(ref, at, n):
        return ref.at[:, pl.ds(at, n)]

    def lines(ref, at, n):
        return ref.at[pl.ds(at, n)]

    c_wia = one(win.at[0, :, pl.ds(0, HA)], columns(wi, RA, HA), p_wgt)
    c_woa = one(wout.at[0, pl.ds(0, HA)], lines(wo, RA, HA), p_wgt)
    c_wib = one(win.at[0, :, pl.ds(HA, HB)], columns(wi, RB, HB), p_wgt)
    c_wob = one(wout.at[0, pl.ds(HA, HB)], lines(wo, RB, HB), p_wgt)
    c_wis = one(win.at[0], columns(wi, SIB, H), p_core)
    c_wos = one(wout.at[0], lines(wo, SIB, H), p_core)
    f_wia = one(columns(wi, RA, HA), columns(wi, RAS, HA), p_core)
    f_woa = one(lines(wo, RA, HA), lines(wo, RAS, HA), p_core)
    f_wib = one(columns(wi, RB, HB), columns(wi, RBS, HB), p_core)
    f_wob = one(lines(wo, RB, HB), lines(wo, RBS, HB), p_core)
    for c in [c_info[1], c_x[1], c_info[0], c_x[0], c_g[1], c_g[0], c_wia]:
        go(c)

    def codes(s):
        shift = (s % 2) * CAP - 1024.0 * z_lo.astype(f32)
        return info[s, 0:2, :] + shift

    def build(s):
        code = codes(s)
        g, at = s // 2, s % 2
        row = lax.broadcasted_iota(jnp.int32, (G, T), 0).astype(f32)
        hit = jnp.logical_or(row == code[0:1, :], row == code[1:2, :])
        pk[g * G : (g + 1) * G, at * T : (at + 1) * T] = jnp.where(hit, 1.0, 0.0).astype(bf16)
        lane = lax.broadcasted_iota(jnp.int32, (T, G), 1).astype(f32)
        hit = jnp.logical_or(lane == to_col(code[0:1, :]), lane == to_col(code[1:2, :]))
        pt[s * T : (s + 1) * T, :] = jnp.where(hit, 1.0, 0.0).astype(bf16)

    tile = G // 2

    def pack_x(g):
        raw = xraw[g * 2 * T : (g + 1) * 2 * T, :]
        for i in range(2):
            at = g * G + i * tile
            put_rows(xpk, g * Q + i * Q // 2, Q // 2, dot(pk[at : at + tile, :], raw))

    def pack_g(g):
        raw = graw[g * 2 * T : (g + 1) * 2 * T, :]
        for i in range(2):
            at = g * G + i * tile
            row = (lax.broadcasted_iota(jnp.int32, (tile, T), 0) + i * tile).astype(f32)
            gate = jnp.zeros((tile, T), f32)
            for s in (2 * g, 2 * g + 1):
                code = codes(s)
                for k in range(2):
                    gate += jnp.where(row == code[k : k + 1, :], info[s, 2 + k : 3 + k, :], 0.0)
            gate = jnp.sum(gate, axis=1, keepdims=True)
            put_rows(gpk, g * Q + i * Q // 2, Q // 2, dot(pk[at : at + tile, :], raw) * gate)

    build(0)
    for c in copies[:2]:
        c.wait()
    c_info[0].wait_recv()
    build(1)
    c_x[0].wait_recv()
    pack_x(0)
    send_all(xpk, xrv, sx, rx, 0, 6)
    c_info[1].wait_recv()
    go(f_info)
    c_x[1].wait_recv()
    go(f_x)
    for c in (c_woa, c_wis, c_wos):
        go(c)
    build(2)
    c_g[0].wait_recv()
    pack_g(0)
    send_all(gpk, grv, sg, rgs, 0, 8)
    c_g[1].wait_recv()
    go(f_g)
    for c in (c_wib, c_wob):
        go(c)
    f_info.wait_recv()
    build(3)
    f_x.wait_recv()
    pack_x(1)
    send_all(xpk, xrv, sx, rx, 1, 6)
    f_g.wait_recv()
    pack_g(1)
    send_all(gpk, grv, sg, rgs, 1, 8)

    def slopes(at, n):
        @pl.loop(0, 2)
        def _(g):
            rows = pl.ds(pl.multiple_of(g * G, G), G)
            sl[rows, at : at + n] = gelu_slope(dot(rows_of(xrv, g * Q, Q), wi[:, at : at + n]))

    def grads(at, n, g):
        rows = slice(g * G, (g + 1) * G)
        act = dot_t(rows_of(grv, g * Q, Q), wo[at : at + n, :])
        pg[rows, at : at + n] = (act * sl[rows, at : at + n]).astype(bf16)

    copies[2].wait()
    c_wis.wait_recv()
    for g in range(2):
        wait_all(xpk, xrv, sx, rx, g, 6)
    slopes(OWN, 2 * H)
    xt[...] = rows_of(xrv, 0, 2 * Q).T
    c_wia.wait_recv()
    go(f_wia)
    f_wia.wait_recv()
    slopes(RA, 2 * HA)
    copies[3].wait()
    c_wos.wait_recv()
    wait_all(gpk, grv, sg, rgs, 0, 8)
    grads(OWN, 2 * H, 0)
    c_woa.wait_recv()
    go(f_woa)
    c_wib.wait_recv()
    go(f_wib)
    f_woa.wait_recv()
    grads(RA, 2 * HA, 0)
    f_wib.wait_recv()
    slopes(RB, 2 * HB)
    wait_all(gpk, grv, sg, rgs, 1, 8)
    grads(RA, 2 * HA, 1)

    c_ga = one(wsa, wra, p_core)
    c_gb = one(wsb, wrb, p_core)
    c_gc = one(wsc, wrc, p_core)
    c_za = one(za, zra, p_wgt)
    c_zb = one(zb, zrb, p_wgt)

    def partial_grad(at, n, kept, sent):
        @pl.loop(0, D // H)
        def _(i):
            rows = pl.ds(pl.multiple_of(i * H, H), H)
            part = dot(xt[rows, :], pg[:, at : at + 2 * n])
            kept[rows, :] = part[:, 0:n]
            sent[rows, :] = part[:, n : 2 * n].astype(bf16)

    partial_grad(RA, HA, wgr.at[:, 0:HA], wsa)
    go(c_ga)
    c_wob.wait_recv()
    go(f_wob)
    grads(OWN, 2 * H, 1)
    c_ga.wait_recv()
    za[...] = (wgr[:, 0:HA] + wra[...].astype(f32)).astype(bf16)
    go(c_za)
    f_wob.wait_recv()
    grads(RB, 2 * HB, 1)
    grads(RB, 2 * HB, 0)

    for g in (1, 0):
        put_rows(rg, g * Q, Q, dot_t(pg[g * G : (g + 1) * G, :], wi[...]))
        send_all(rg, rt, st, rts, g, 10)
    partial_grad(RB, HB, wgr.at[:, HA:H], wsb)
    go(c_gb)
    partial_grad(OWN, H, wg, wsc)
    go(c_gc)
    c_gb.wait_recv()
    zb[...] = (wgr[:, HA:H] + wrb[...].astype(f32)).astype(bf16)
    go(c_zb)
    c_gc.wait_recv()
    for c in copies[4:]:
        c.wait()

    def adam(at, n, arrived):
        cols = slice(at, at + n)
        grad = wg[:, cols] + wrc[:, cols].astype(f32) + arrived[...].astype(f32)
        first = beta_one * mm1[:, cols] + (1.0 - beta_one) * grad
        second = beta_two * mm2[:, cols] + (1.0 - beta_two) * grad * grad
        step = (first / (1.0 - beta_one**ADAM_STEP)) / (
            jnp.sqrt(second / (1.0 - beta_two**ADAM_STEP)) + adam_eps
        )
        an[:, cols] = step.astype(bf16)

    c_swa = one(columns(an, 0, HA), columns(ar, 0, HA), p_zlo)
    c_swb = one(columns(an, HA, HB), columns(ar, HA, HB), p_zlo)
    c_z1 = one(zs.at[pl.ds(T, T)], zr.at[pl.ds(T, T)], p_zlo)
    c_z0 = one(zs.at[pl.ds(0, T)], zr.at[pl.ds(0, T)], p_zlo)
    c_back = one(xs, xr, p_row)
    outs = [
        local(12, columns(an, 0, HA), columns(ao, 0, HA)),
        local(13, columns(an, HA, HB), columns(ao, HA, HB)),
        local(14, keep.at[pl.ds(0, T)], xp),
    ]

    def combine(s):
        return dot(pt[s * T : (s + 1) * T, :], rows_of(rt, (s // 2) * Q, Q))

    wait_all(rg, rt, st, rts, 1, 10)
    zs[T : 2 * T, :] = combine(3).astype(bf16)
    go(c_z1)
    keep[T : 2 * T, :] = combine(2)
    wait_all(rg, rt, st, rts, 0, 10)
    zs[0:T, :] = combine(1).astype(bf16)
    go(c_z0)
    keep[0:T, :] = combine(0)
    c_za.wait_recv()
    adam(0, HA, zra)
    c_swa.start()
    outs[0].start()
    c_z1.wait_recv()
    xs[...] = (keep[T : 2 * T, :] + zr[T : 2 * T, :].astype(f32)).astype(bf16)
    c_back.start()
    c_zb.wait_recv()
    adam(HA, HB, zrb)
    c_swb.start()
    outs[1].start()
    c_z0.wait_recv()
    keep[0:T, :] += zr[0:T, :].astype(f32)
    outs[2].start()

    @pl.loop(1, Q)
    def _(d):
        for g in range(2):
            send(xpk, xrv, sx, rx, g, d).wait_send()
            send(gpk, grv, sg, rgs, g, d).wait_send()
            send(rg, rt, st, rts, g, d).wait_send()

    for c in started:
        c.wait_send()
    for c in (c_swa, c_back, c_swb, *outs):
        c.wait()


def finish(swp, xp, xr, an, ar, xo, ao):
    e = lax.axis_index("expert")
    expert = lax.broadcasted_iota(jnp.int32, (1, E), 1)
    new_home = jnp.sum(jnp.where(expert == e, swp[...].astype(f32), 0.0), axis=1, keepdims=True)
    moved = jnp.broadcast_to(new_home != e.astype(f32), (ao.shape[0], T))
    for i in range(0, H, T):
        ao[:, i : i + T] = jnp.where(moved, ar[:, i : i + T], an[:, i : i + T])
    xo[...] = (xp[...] + xr[...].astype(f32)).astype(bf16)


def shards(tokens, out_grad, gates, expert_ids, swap_list, w_in, w_out, first_moment, second_moment):
    any_spec = pl.BlockSpec(memory_space=pl.ANY)
    vmem = pl.BlockSpec(memory_space=pltpu.VMEM)
    dma = pltpu.SemaphoreType.DMA
    xp, xr, an, ar = pl.pallas_call(
        kernel,
        out_shape=(
            jax.ShapeDtypeStruct((T, D), f32),
            jax.ShapeDtypeStruct((T, D), bf16),
            jax.ShapeDtypeStruct((D, H), bf16),
            jax.ShapeDtypeStruct((D, H), bf16),
        ),
        in_specs=[any_spec, any_spec, vmem, vmem, any_spec, any_spec, any_spec, any_spec],
        out_specs=(any_spec, any_spec, any_spec, any_spec),
        scratch_shapes=[
            pltpu.VMEM((4, 8, T), f32),
            pltpu.VMEM((4 * T, D), bf16),
            pltpu.VMEM((4 * T, D), bf16),
            pltpu.VMEM((R, 2 * T), bf16),
            pltpu.VMEM((4 * T, G), bf16),
            pltpu.VMEM((2 * Q, B, D), bf16),
            pltpu.VMEM((2 * Q, B, D), bf16),
            pltpu.VMEM((2 * Q, B, D), bf16),
            pltpu.VMEM((2 * Q, B, D), bf16),
            pltpu.VMEM((D, R), bf16),
            pltpu.VMEM((R, 4 * H), f32),
            pltpu.VMEM((D, 4 * H), bf16),
            pltpu.VMEM((4 * H, D), bf16),
            pltpu.VMEM((R, 4 * H), bf16),
            pltpu.VMEM((2 * Q, B, D), bf16),
            pltpu.VMEM((2 * Q, B, D), bf16),
            pltpu.VMEM((D, H), f32),
            pltpu.VMEM((D, H), f32),
            pltpu.VMEM((D, HA), bf16),
            pltpu.VMEM((D, HA), bf16),
            pltpu.VMEM((D, HB), bf16),
            pltpu.VMEM((D, HB), bf16),
            pltpu.VMEM((D, H), bf16),
            pltpu.VMEM((D, H), bf16),
            pltpu.VMEM((D, HA), bf16),
            pltpu.VMEM((D, HA), bf16),
            pltpu.VMEM((D, HB), bf16),
            pltpu.VMEM((D, HB), bf16),
            pltpu.VMEM((D, H), f32),
            pltpu.VMEM((D, H), f32),
            pltpu.VMEM((2 * T, D), bf16),
            pltpu.VMEM((2 * T, D), bf16),
            pltpu.VMEM((T, D), bf16),
            pltpu.VMEM((2 * T, D), f32),
            pltpu.VMEM((D, H), bf16),
            dma((N_ONE,)), dma((N_ONE,)), dma((N_LOCAL,)),
            dma((E,)), dma((E,)), dma((E,)), dma((E,)), dma((E,)), dma((E,)),
        ],
        compiler_params=pltpu.CompilerParams(
            collective_id=0, has_side_effects=True, vmem_limit_bytes=60 << 20
        ),
        name="experts",
    )(tokens, out_grad, expert_ids.T, gates.T, w_in, w_out, first_moment, second_moment)
    steps = 2
    rows = pl.BlockSpec((T // steps, D), lambda i: (i, 0))
    block = pl.BlockSpec((D // steps, H), lambda i: (i, 0))
    x_grad, adam_out = pl.pallas_call(
        finish,
        grid=(steps,),
        out_shape=(jax.ShapeDtypeStruct((T, D), bf16), jax.ShapeDtypeStruct((D, H), bf16)),
        in_specs=[pl.BlockSpec((1, E), lambda i: (0, 0)), rows, rows, block, block],
        out_specs=(rows, block),
        name="finish",
    )(swap_list[None], xp, xr, an, ar)
    return x_grad, adam_out[None]


def solution(mesh):
    token_spec = P(("dp", "expert"), None)
    in_specs = (
        token_spec, token_spec, token_spec, token_spec, P(),
        P("expert", None, "dp"), P("expert", "dp", None), P("expert", None, "dp"), P("expert", None, "dp"),
    )
    out_specs = (token_spec, P("expert", None, "dp"))
    return jax.shard_map(shards, mesh=mesh, in_specs=in_specs, out_specs=out_specs, check_vma=False)
```

```python
import jax
import jax.numpy as jnp
from jax import lax
from jax.experimental import pallas as pl
from jax.experimental.pallas import tpu as pltpu
from jax.sharding import PartitionSpec as P

ADAM_STEP = 100
coef_c = 0.7978845608028654
coef_a = 0.044715
beta_one = 0.9
beta_two = 0.999
adam_eps = 1e-08

D = 1152
H = 384
T = 128
E = 32
Q = 16
CAP = 12
B = 2 * CAP
G = Q * B
R = 2 * G
HA, HB = 256, 128
MESH = pl.DeviceIdType.MESH
f32, bf16 = jnp.float32, jnp.bfloat16

OWN, SIB, RA, RAS, RB, RBS = 0, H, 2 * H, 2 * H + HA, 2 * H + 2 * HA, 2 * H + 2 * HA + HB
N_ONE = 40
N_LOCAL = 15


def gelu_slope(u):
    h = jnp.tanh(coef_c * (u + coef_a * u * u * u))
    return 0.5 * (1.0 + h) + 0.5 * u * (1.0 - h * h) * coef_c * (
        1.0 + 3.0 * coef_a * u * u
    )


def dot(a, b):
    return jnp.dot(a, b, preferred_element_type=f32)


def dot_t(a, b):
    return lax.dot_general(a, b, (((1,), (1,)), ((), ())), preferred_element_type=f32)


def kernel(
    tok, og, ids, gts, win, wout, m1, m2,
    xp, xr, ao, ar,
    info, xraw, graw, pk, pt, xpk, gpk, xrv, grv, xt, sl, wi, wo, pg, rg, rt,
    wg, wgr, wsa, wra, wsb, wrb, wsc, wrc, za, zra, zb, zrb, mm1, mm2, zs, zr, zd, xs, keep, an,
    s1, r1, lo, sx, rx, sg, rgs, st, rts,
):
    dp, e = lax.axis_index("dp"), lax.axis_index("expert")
    zh, core = dp // 2, dp % 2
    z_lo, y, x = e // Q, (e // 4) % 4, e % 4
    me = e % Q
    p_row = ((zh + 1 - 2 * (zh % 2)) * 2 + core, e)
    p_wgt = ((3 - zh) * 2 + core, e)
    p_core = (zh * 2 + 1 - core, e)
    p_zlo = (dp, (e + Q) % E)
    p_diag = ((zh + 1 - 2 * (zh % 2)) * 2 + core, (e + Q) % E)
    inner = (zh % 2 + z_lo) == 1
    outer = (zh % 2 + z_lo) != 1
    used = []
    started = []

    def one(src, dst, dev):
        used.append(None)
        i = len(used) - 1
        return pltpu.make_async_remote_copy(
            src_ref=src, dst_ref=dst, send_sem=s1.at[i], recv_sem=r1.at[i], device_id=dev, device_id_type=MESH
        )

    def go(copy):
        copy.start()
        started.append(copy)

    def local(i, src, dst):
        return pltpu.make_async_copy(src, dst, lo.at[i])

    def rows_of(ref, at, n):
        return ref[pl.ds(at, n)].reshape(n * B, D)

    def put_rows(ref, at, n, value):
        ref[pl.ds(at, n)] = value.astype(bf16).reshape(n, B, D)

    def peer(d, sign):
        a, b = d % 4, d // 4
        return ((y + 4 + sign * ((a + b) % 4)) % 4) * 4 + (x + 4 + sign * a) % 4

    def send(src, dst, ss, rs, g, d):
        q = peer(d, 1)
        return pltpu.make_async_remote_copy(
            src_ref=src.at[g * Q + q], dst_ref=dst.at[g * Q + me], send_sem=ss.at[g * Q + d],
            recv_sem=rs.at[g * Q + d], device_id=(dp, z_lo * Q + q), device_id_type=MESH,
        )

    def arrival(src, dst, ss, rs, g, d):
        q = peer(d, -1)
        return pltpu.make_async_remote_copy(
            src_ref=src.at[g * Q + q], dst_ref=dst.at[g * Q + q], send_sem=ss.at[g * Q + d],
            recv_sem=rs.at[g * Q + d], device_id=(dp, z_lo * Q + q), device_id_type=MESH,
        )

    def own_block(i, src, dst, g):
        return local(i + g, src.at[g * Q + me], dst.at[g * Q + me])

    def send_all(src, dst, ss, rs, g, i):
        own_block(i, src, dst, g).start()

        @pl.loop(1, Q)
        def _(d):
            send(src, dst, ss, rs, g, d).start()

    def wait_all(src, dst, ss, rs, g, i):
        own_block(i, src, dst, g).wait()

        @pl.loop(1, Q)
        def _(d):
            arrival(src, dst, ss, rs, g, d).wait_recv()

    copies = [
        local(0, tok, xraw.at[pl.ds(0, T)]),
        local(1, og, graw.at[pl.ds(0, T)]),
        local(2, win.at[0], wi.at[:, pl.ds(OWN, H)]),
        local(3, wout.at[0], wo.at[pl.ds(OWN, H)]),
        local(4, m1.at[0], mm1),
        local(5, m2.at[0], mm2),
    ]
    for c in copies:
        c.start()

    iota_r = lax.broadcasted_iota(jnp.int32, (T, T), 0)
    iota_c = lax.broadcasted_iota(jnp.int32, (T, T), 1)
    eye, before = iota_r == iota_c, iota_r < iota_c
    idr = [ids[k : k + 1, :].astype(f32) for k in range(2)]

    def to_col(row):
        return jnp.sum(jnp.where(eye, row, 0.0), axis=1, keepdims=True)

    idc = [to_col(r) for r in idr]

    def count(k, j, mask):
        same = idc[k] == idr[j]
        same = jnp.logical_and(same, mask) if mask is not None else same
        return jnp.sum(jnp.where(same, 1.0, 0.0), axis=0, keepdims=True)

    ranks = [count(0, 0, before), count(0, 1, None) + count(1, 1, before)]
    for k in range(2):
        high = jnp.where(idr[k] >= float(Q), 1.0, 0.0)
        info[0, k : k + 1, :] = high * 1024.0 + (idr[k] - high * Q) * float(B) + ranks[k]
    info[0, 2:4, :] = gts[...]
    info[0, 4:8, :] = jnp.zeros((4, T), f32)

    barrier = pltpu.get_barrier_semaphore()
    for dev in (p_row, p_wgt, p_core, p_zlo, p_diag):
        pl.semaphore_signal(barrier, inc=1, device_id=dev, device_id_type=MESH)

    @pl.loop(1, Q)
    def _(d):
        pl.semaphore_signal(barrier, inc=1, device_id=(dp, z_lo * Q + peer(d, 1)), device_id_type=MESH)

    pl.semaphore_wait(barrier, Q + 4)

    def source(ref, s):
        return ref.at[pl.ds(s * T, T)]

    c_info = [one(info.at[0], info.at[1], p_zlo), one(info.at[0], info.at[2], p_row)]
    c_x = [one(tok, source(xraw, 1), p_zlo), one(tok, source(xraw, 2), p_row)]
    c_g = [one(og, source(graw, 1), p_zlo), one(og, source(graw, 2), p_row)]
    f_info = one(info.at[2], info.at[3], p_zlo)
    f_x = one(source(xraw, 2), source(xraw, 3), p_zlo)
    f_g = one(source(graw, 2), source(graw, 3), p_zlo)

    d_info = one(info.at[0], info.at[3], p_diag)
    d_x = one(tok, source(xraw, 3), p_diag)
    d_g = one(og, source(graw, 3), p_diag)

    def inner_go(*copies_out):
        @pl.when(inner)
        def _():
            for c in copies_out:
                c.start()

    def wait_diag(direct, passed):
        @pl.when(inner)
        def _():
            direct.wait_recv()

        @pl.when(outer)
        def _():
            passed.wait_recv()

    def columns(ref, at, n):
        return ref.at[:, pl.ds(at, n)]

    def lines(ref, at, n):
        return ref.at[pl.ds(at, n)]

    c_wia = one(win.at[0, :, pl.ds(0, HA)], columns(wi, RA, HA), p_wgt)
    c_woa = one(wout.at[0, pl.ds(0, HA)], lines(wo, RA, HA), p_wgt)
    c_wib = one(win.at[0, :, pl.ds(HA, HB)], columns(wi, RB, HB), p_wgt)
    c_wob = one(wout.at[0, pl.ds(HA, HB)], lines(wo, RB, HB), p_wgt)
    c_wis = one(win.at[0], columns(wi, SIB, H), p_core)
    c_wos = one(wout.at[0], lines(wo, SIB, H), p_core)
    f_wia = one(columns(wi, RA, HA), columns(wi, RAS, HA), p_core)
    f_woa = one(lines(wo, RA, HA), lines(wo, RAS, HA), p_core)
    f_wib = one(columns(wi, RB, HB), columns(wi, RBS, HB), p_core)
    f_wob = one(lines(wo, RB, HB), lines(wo, RBS, HB), p_core)
    for c in [c_info[1], c_x[1], c_info[0], c_x[0], c_g[1], c_g[0]]:
        go(c)
    inner_go(d_info, d_x, d_g)
    go(c_wia)

    def codes(s):
        shift = (s % 2) * CAP - 1024.0 * z_lo.astype(f32)
        return info[s, 0:2, :] + shift

    def build(s):
        code = codes(s)
        g, at = s // 2, s % 2
        row = lax.broadcasted_iota(jnp.int32, (G, T), 0).astype(f32)
        hit = jnp.logical_or(row == code[0:1, :], row == code[1:2, :])
        pk[g * G : (g + 1) * G, at * T : (at + 1) * T] = jnp.where(hit, 1.0, 0.0).astype(bf16)
        lane = lax.broadcasted_iota(jnp.int32, (T, G), 1).astype(f32)
        hit = jnp.logical_or(lane == to_col(code[0:1, :]), lane == to_col(code[1:2, :]))
        pt[s * T : (s + 1) * T, :] = jnp.where(hit, 1.0, 0.0).astype(bf16)

    tile = G // 2

    def pack_x(g):
        raw = xraw[g * 2 * T : (g + 1) * 2 * T, :]
        for i in range(2):
            at = g * G + i * tile
            put_rows(xpk, g * Q + i * Q // 2, Q // 2, dot(pk[at : at + tile, :], raw))

    def pack_g(g):
        raw = graw[g * 2 * T : (g + 1) * 2 * T, :]
        for i in range(2):
            at = g * G + i * tile
            row = (lax.broadcasted_iota(jnp.int32, (tile, T), 0) + i * tile).astype(f32)
            gate = jnp.zeros((tile, T), f32)
            for s in (2 * g, 2 * g + 1):
                code = codes(s)
                for k in range(2):
                    gate += jnp.where(row == code[k : k + 1, :], info[s, 2 + k : 3 + k, :], 0.0)
            gate = jnp.sum(gate, axis=1, keepdims=True)
            put_rows(gpk, g * Q + i * Q // 2, Q // 2, dot(pk[at : at + tile, :], raw) * gate)

    build(0)
    for c in copies[:2]:
        c.wait()
    c_info[0].wait_recv()
    build(1)
    c_x[0].wait_recv()
    pack_x(0)
    send_all(xpk, xrv, sx, rx, 0, 6)
    c_info[1].wait_recv()
    inner_go(f_info)
    c_x[1].wait_recv()
    inner_go(f_x)
    for c in (c_woa, c_wis, c_wos):
        go(c)
    build(2)
    c_g[0].wait_recv()
    pack_g(0)
    send_all(gpk, grv, sg, rgs, 0, 8)
    c_g[1].wait_recv()
    inner_go(f_g)
    for c in (c_wib, c_wob):
        go(c)
    wait_diag(d_info, f_info)
    build(3)
    wait_diag(d_x, f_x)
    pack_x(1)
    send_all(xpk, xrv, sx, rx, 1, 6)
    wait_diag(d_g, f_g)
    pack_g(1)
    send_all(gpk, grv, sg, rgs, 1, 8)

    def slopes(at, n):
        @pl.loop(0, 2)
        def _(g):
            rows = pl.ds(pl.multiple_of(g * G, G), G)
            sl[rows, at : at + n] = gelu_slope(dot(rows_of(xrv, g * Q, Q), wi[:, at : at + n]))

    def grads(at, n, g):
        rows = slice(g * G, (g + 1) * G)
        act = dot_t(rows_of(grv, g * Q, Q), wo[at : at + n, :])
        pg[rows, at : at + n] = (act * sl[rows, at : at + n]).astype(bf16)

    copies[2].wait()
    c_wis.wait_recv()
    for g in range(2):
        wait_all(xpk, xrv, sx, rx, g, 6)
    slopes(OWN, 2 * H)
    xt[...] = rows_of(xrv, 0, 2 * Q).T
    c_wia.wait_recv()
    go(f_wia)
    f_wia.wait_recv()
    slopes(RA, 2 * HA)
    copies[3].wait()
    c_wos.wait_recv()
    wait_all(gpk, grv, sg, rgs, 0, 8)
    grads(OWN, 2 * H, 0)
    c_woa.wait_recv()
    go(f_woa)
    c_wib.wait_recv()
    go(f_wib)
    f_woa.wait_recv()
    grads(RA, 2 * HA, 0)
    f_wib.wait_recv()
    slopes(RB, 2 * HB)
    wait_all(gpk, grv, sg, rgs, 1, 8)
    grads(RA, 2 * HA, 1)

    c_ga = one(wsa, wra, p_core)
    c_gb = one(wsb, wrb, p_core)
    c_gc = one(wsc, wrc, p_core)
    c_za = one(za, zra, p_wgt)
    c_zb = one(zb, zrb, p_wgt)

    def partial_grad(at, n, kept, sent):
        @pl.loop(0, D // H)
        def _(i):
            rows = pl.ds(pl.multiple_of(i * H, H), H)
            part = dot(xt[rows, :], pg[:, at : at + 2 * n])
            kept[rows, :] = part[:, 0:n]
            sent[rows, :] = part[:, n : 2 * n].astype(bf16)

    partial_grad(RA, HA, wgr.at[:, 0:HA], wsa)
    go(c_ga)
    c_wob.wait_recv()
    go(f_wob)
    grads(OWN, 2 * H, 1)
    c_ga.wait_recv()
    za[...] = (wgr[:, 0:HA] + wra[...].astype(f32)).astype(bf16)
    go(c_za)
    f_wob.wait_recv()
    grads(RB, 2 * HB, 1)
    grads(RB, 2 * HB, 0)

    for g in (1, 0):
        put_rows(rg, g * Q, Q, dot_t(pg[g * G : (g + 1) * G, :], wi[...]))
        send_all(rg, rt, st, rts, g, 10)
    partial_grad(RB, HB, wgr.at[:, HA:H], wsb)
    go(c_gb)
    partial_grad(OWN, H, wg, wsc)
    go(c_gc)
    c_gb.wait_recv()
    zb[...] = (wgr[:, HA:H] + wrb[...].astype(f32)).astype(bf16)
    go(c_zb)
    c_gc.wait_recv()
    for c in copies[4:]:
        c.wait()

    def adam(at, n, arrived):
        cols = slice(at, at + n)
        grad = wg[:, cols] + wrc[:, cols].astype(f32) + arrived[...].astype(f32)
        first = beta_one * mm1[:, cols] + (1.0 - beta_one) * grad
        second = beta_two * mm2[:, cols] + (1.0 - beta_two) * grad * grad
        step = (first / (1.0 - beta_one**ADAM_STEP)) / (
            jnp.sqrt(second / (1.0 - beta_two**ADAM_STEP)) + adam_eps
        )
        an[:, cols] = step.astype(bf16)

    c_swa = one(columns(an, 0, HA), columns(ar, 0, HA), p_zlo)
    c_swb = one(columns(an, HA, HB), columns(ar, HA, HB), p_zlo)
    c_z1 = one(zs.at[pl.ds(T, T)], zr.at[pl.ds(T, T)], p_zlo)
    c_zd = one(zs.at[pl.ds(T, T)], zd, p_diag)
    c_z0 = one(zs.at[pl.ds(0, T)], zr.at[pl.ds(0, T)], p_zlo)
    c_back = one(xs, xr, p_row)
    outs = [
        local(12, columns(an, 0, HA), columns(ao, 0, HA)),
        local(13, columns(an, HA, HB), columns(ao, HA, HB)),
        local(14, keep.at[pl.ds(0, T)], xp),
    ]

    def combine(s):
        return dot(pt[s * T : (s + 1) * T, :], rows_of(rt, (s // 2) * Q, Q))

    wait_all(rg, rt, st, rts, 1, 10)
    zs[T : 2 * T, :] = combine(3).astype(bf16)

    @pl.when(inner)
    def _():
        c_zd.start()

    @pl.when(outer)
    def _():
        c_z1.start()

    keep[T : 2 * T, :] = combine(2)

    @pl.when(outer)
    def _():
        xs[...] = keep[T : 2 * T, :].astype(bf16)
        c_back.start()

    wait_all(rg, rt, st, rts, 0, 10)
    zs[0:T, :] = combine(1).astype(bf16)
    go(c_z0)
    keep[0:T, :] = combine(0)
    c_za.wait_recv()
    adam(0, HA, zra)
    c_swa.start()
    outs[0].start()

    @pl.when(inner)
    def _():
        c_z1.wait_recv()
        xs[...] = (keep[T : 2 * T, :] + zr[T : 2 * T, :].astype(f32)).astype(bf16)
        c_back.start()

    c_zb.wait_recv()
    adam(HA, HB, zrb)
    c_swb.start()
    outs[1].start()
    c_z0.wait_recv()
    keep[0:T, :] += zr[0:T, :].astype(f32)

    @pl.when(inner)
    def _():
        c_zd.wait_recv()
        keep[0:T, :] += zd[...].astype(f32)

    outs[2].start()

    @pl.loop(1, Q)
    def _(d):
        for g in range(2):
            send(xpk, xrv, sx, rx, g, d).wait_send()
            send(gpk, grv, sg, rgs, g, d).wait_send()
            send(rg, rt, st, rts, g, d).wait_send()

    for c in started:
        c.wait_send()

    @pl.when(inner)
    def _():
        for c in (d_info, d_x, d_g, f_info, f_x, f_g, c_zd):
            c.wait_send()

    @pl.when(outer)
    def _():
        c_z1.wait_send()

    for c in (c_swa, c_back, c_swb, *outs):
        c.wait()


def finish(swp, xp, xr, an, ar, xo, ao):
    e = lax.axis_index("expert")
    expert = lax.broadcasted_iota(jnp.int32, (1, E), 1)
    new_home = jnp.sum(jnp.where(expert == e, swp[...].astype(f32), 0.0), axis=1, keepdims=True)
    moved = jnp.broadcast_to(new_home != e.astype(f32), (ao.shape[0], T))
    for i in range(0, H, T):
        ao[:, i : i + T] = jnp.where(moved, ar[:, i : i + T], an[:, i : i + T])
    xo[...] = (xp[...] + xr[...].astype(f32)).astype(bf16)


def shards(tokens, out_grad, gates, expert_ids, swap_list, w_in, w_out, first_moment, second_moment):
    any_spec = pl.BlockSpec(memory_space=pl.ANY)
    vmem = pl.BlockSpec(memory_space=pltpu.VMEM)
    dma = pltpu.SemaphoreType.DMA
    xp, xr, an, ar = pl.pallas_call(
        kernel,
        out_shape=(
            jax.ShapeDtypeStruct((T, D), f32),
            jax.ShapeDtypeStruct((T, D), bf16),
            jax.ShapeDtypeStruct((D, H), bf16),
            jax.ShapeDtypeStruct((D, H), bf16),
        ),
        in_specs=[any_spec, any_spec, vmem, vmem, any_spec, any_spec, any_spec, any_spec],
        out_specs=(any_spec, any_spec, any_spec, any_spec),
        scratch_shapes=[
            pltpu.VMEM((4, 8, T), f32),
            pltpu.VMEM((4 * T, D), bf16),
            pltpu.VMEM((4 * T, D), bf16),
            pltpu.VMEM((R, 2 * T), bf16),
            pltpu.VMEM((4 * T, G), bf16),
            pltpu.VMEM((2 * Q, B, D), bf16),
            pltpu.VMEM((2 * Q, B, D), bf16),
            pltpu.VMEM((2 * Q, B, D), bf16),
            pltpu.VMEM((2 * Q, B, D), bf16),
            pltpu.VMEM((D, R), bf16),
            pltpu.VMEM((R, 4 * H), f32),
            pltpu.VMEM((D, 4 * H), bf16),
            pltpu.VMEM((4 * H, D), bf16),
            pltpu.VMEM((R, 4 * H), bf16),
            pltpu.VMEM((2 * Q, B, D), bf16),
            pltpu.VMEM((2 * Q, B, D), bf16),
            pltpu.VMEM((D, H), f32),
            pltpu.VMEM((D, H), f32),
            pltpu.VMEM((D, HA), bf16),
            pltpu.VMEM((D, HA), bf16),
            pltpu.VMEM((D, HB), bf16),
            pltpu.VMEM((D, HB), bf16),
            pltpu.VMEM((D, H), bf16),
            pltpu.VMEM((D, H), bf16),
            pltpu.VMEM((D, HA), bf16),
            pltpu.VMEM((D, HA), bf16),
            pltpu.VMEM((D, HB), bf16),
            pltpu.VMEM((D, HB), bf16),
            pltpu.VMEM((D, H), f32),
            pltpu.VMEM((D, H), f32),
            pltpu.VMEM((2 * T, D), bf16),
            pltpu.VMEM((2 * T, D), bf16),
            pltpu.VMEM((T, D), bf16),
            pltpu.VMEM((T, D), bf16),
            pltpu.VMEM((2 * T, D), f32),
            pltpu.VMEM((D, H), bf16),
            dma((N_ONE,)), dma((N_ONE,)), dma((N_LOCAL,)),
            dma((E,)), dma((E,)), dma((E,)), dma((E,)), dma((E,)), dma((E,)),
        ],
        compiler_params=pltpu.CompilerParams(
            collective_id=0, has_side_effects=True, vmem_limit_bytes=60 << 20
        ),
        name="experts",
    )(tokens, out_grad, expert_ids.T, gates.T, w_in, w_out, first_moment, second_moment)
    steps = 2
    rows = pl.BlockSpec((T // steps, D), lambda i: (i, 0))
    block = pl.BlockSpec((D // steps, H), lambda i: (i, 0))
    x_grad, adam_out = pl.pallas_call(
        finish,
        grid=(steps,),
        out_shape=(jax.ShapeDtypeStruct((T, D), bf16), jax.ShapeDtypeStruct((D, H), bf16)),
        in_specs=[pl.BlockSpec((1, E), lambda i: (0, 0)), rows, rows, block, block],
        out_specs=(rows, block),
        name="finish",
    )(swap_list[None], xp, xr, an, ar)
    return x_grad, adam_out[None]


def solution(mesh):
    token_spec = P(("dp", "expert"), None)
    in_specs = (
        token_spec, token_spec, token_spec, token_spec, P(),
        P("expert", None, "dp"), P("expert", "dp", None), P("expert", None, "dp"), P("expert", None, "dp"),
    )
    out_specs = (token_spec, P("expert", None, "dp"))
    return jax.shard_map(shards, mesh=mesh, in_specs=in_specs, out_specs=out_specs, check_vma=False)
```

```python
import jax
import jax.numpy as jnp
from jax import lax
from jax.experimental import pallas as pl
from jax.experimental.pallas import tpu as pltpu
from jax.sharding import PartitionSpec as P

ADAM_STEP = 100
coef_c = 0.7978845608028654
coef_a = 0.044715
beta_one = 0.9
beta_two = 0.999
adam_eps = 1e-08

D = 1152
H = 384
T = 128
E = 32
Q = 16
CAP = 12
B = 2 * CAP
G = Q * B
R = 2 * G
HA, HB = 256, 128
MESH = pl.DeviceIdType.MESH
f32, bf16 = jnp.float32, jnp.bfloat16

OWN, SIB, RA, RAS, RB, RBS = 0, H, 2 * H, 2 * H + HA, 2 * H + 2 * HA, 2 * H + 2 * HA + HB
N_ONE = 40
N_LOCAL = 15


def gelu_slope(u):
    h = jnp.tanh(coef_c * (u + coef_a * u * u * u))
    return 0.5 * (1.0 + h) + 0.5 * u * (1.0 - h * h) * coef_c * (
        1.0 + 3.0 * coef_a * u * u
    )


def dot(a, b):
    return jnp.dot(a, b, preferred_element_type=f32)


def dot_t(a, b):
    return lax.dot_general(a, b, (((1,), (1,)), ((), ())), preferred_element_type=f32)


def kernel(
    tok, og, ids, gts, win, wout, m1, m2,
    xp, xr, ao, ar,
    info, xraw, graw, pk, pt, xpk, gpk, xrv, grv, xt, sl, wi, wo, pg, rg, rt,
    wg, wgr, wsa, wra, wsb, wrb, wsc, wrc, za, zra, zb, zrb, mm1, mm2, zs, zr, zd, xs, keep, an,
    s1, r1, lo, sx, rx, sg, rgs, st, rts,
):
    dp, e = lax.axis_index("dp"), lax.axis_index("expert")
    zh, core = dp // 2, dp % 2
    z_lo, y, x = e // Q, (e // 4) % 4, e % 4
    me = e % Q
    p_row = ((zh + 1 - 2 * (zh % 2)) * 2 + core, e)
    p_wgt = ((3 - zh) * 2 + core, e)
    p_core = (zh * 2 + 1 - core, e)
    p_zlo = (dp, (e + Q) % E)
    p_diag = ((zh + 1 - 2 * (zh % 2)) * 2 + core, (e + Q) % E)
    inner = (zh % 2 + z_lo) == 1
    outer = (zh % 2 + z_lo) != 1
    used = []
    started = []

    def one(src, dst, dev):
        used.append(None)
        i = len(used) - 1
        return pltpu.make_async_remote_copy(
            src_ref=src, dst_ref=dst, send_sem=s1.at[i], recv_sem=r1.at[i], device_id=dev, device_id_type=MESH
        )

    def go(copy):
        copy.start()
        started.append(copy)

    def local(i, src, dst):
        return pltpu.make_async_copy(src, dst, lo.at[i])

    def rows_of(ref, at, n):
        return ref[pl.ds(at, n)].reshape(n * B, D)

    def put_rows(ref, at, n, value):
        ref[pl.ds(at, n)] = value.astype(bf16).reshape(n, B, D)

    def peer(d, sign):
        a, b = d % 4, d // 4
        return ((y + 4 + sign * ((a + b) % 4)) % 4) * 4 + (x + 4 + sign * a) % 4

    def send(src, dst, ss, rs, g, d):
        q = peer(d, 1)
        return pltpu.make_async_remote_copy(
            src_ref=src.at[g * Q + q], dst_ref=dst.at[g * Q + me], send_sem=ss.at[g * Q + d],
            recv_sem=rs.at[g * Q + d], device_id=(dp, z_lo * Q + q), device_id_type=MESH,
        )

    def arrival(src, dst, ss, rs, g, d):
        q = peer(d, -1)
        return pltpu.make_async_remote_copy(
            src_ref=src.at[g * Q + q], dst_ref=dst.at[g * Q + q], send_sem=ss.at[g * Q + d],
            recv_sem=rs.at[g * Q + d], device_id=(dp, z_lo * Q + q), device_id_type=MESH,
        )

    def own_block(i, src, dst, g):
        return local(i + g, src.at[g * Q + me], dst.at[g * Q + me])

    def send_all(src, dst, ss, rs, g, i):
        own_block(i, src, dst, g).start()

        @pl.loop(1, Q)
        def _(d):
            send(src, dst, ss, rs, g, d).start()

    def wait_all(src, dst, ss, rs, g, i):
        own_block(i, src, dst, g).wait()

        @pl.loop(1, Q)
        def _(d):
            arrival(src, dst, ss, rs, g, d).wait_recv()

    copies = [
        local(0, tok, xraw.at[pl.ds(0, T)]),
        local(1, og, graw.at[pl.ds(0, T)]),
        local(2, win.at[0], wi.at[:, pl.ds(OWN, H)]),
        local(3, wout.at[0], wo.at[pl.ds(OWN, H)]),
        local(4, m1.at[0], mm1),
        local(5, m2.at[0], mm2),
    ]
    for c in copies:
        c.start()

    iota_r = lax.broadcasted_iota(jnp.int32, (T, T), 0)
    iota_c = lax.broadcasted_iota(jnp.int32, (T, T), 1)
    eye, before = iota_r == iota_c, iota_r < iota_c
    idr = [ids[k : k + 1, :].astype(f32) for k in range(2)]

    def to_col(row):
        return jnp.sum(jnp.where(eye, row, 0.0), axis=1, keepdims=True)

    idc = [to_col(r) for r in idr]

    def count(k, j, mask):
        same = idc[k] == idr[j]
        same = jnp.logical_and(same, mask) if mask is not None else same
        return jnp.sum(jnp.where(same, 1.0, 0.0), axis=0, keepdims=True)

    ranks = [count(0, 0, before), count(0, 1, None) + count(1, 1, before)]
    for k in range(2):
        high = jnp.where(idr[k] >= float(Q), 1.0, 0.0)
        info[0, k : k + 1, :] = high * 1024.0 + (idr[k] - high * Q) * float(B) + ranks[k]
    info[0, 2:4, :] = gts[...]
    info[0, 4:8, :] = jnp.zeros((4, T), f32)

    barrier = pltpu.get_barrier_semaphore()
    for dev in (p_row, p_wgt, p_core, p_zlo, p_diag):
        pl.semaphore_signal(barrier, inc=1, device_id=dev, device_id_type=MESH)

    @pl.loop(1, Q)
    def _(d):
        pl.semaphore_signal(barrier, inc=1, device_id=(dp, z_lo * Q + peer(d, 1)), device_id_type=MESH)

    pl.semaphore_wait(barrier, Q + 4)

    def source(ref, s):
        return ref.at[pl.ds(s * T, T)]

    c_info = [one(info.at[0], info.at[1], p_zlo), one(info.at[0], info.at[2], p_row)]
    c_x = [one(tok, source(xraw, 1), p_zlo), one(tok, source(xraw, 2), p_row)]
    c_g = [one(og, source(graw, 1), p_zlo), one(og, source(graw, 2), p_row)]
    f_info = one(info.at[2], info.at[3], p_zlo)
    f_x = one(source(xraw, 2), source(xraw, 3), p_zlo)
    f_g = one(source(graw, 2), source(graw, 3), p_zlo)

    d_info = one(info.at[0], info.at[3], p_diag)
    d_x = one(tok, source(xraw, 3), p_diag)
    d_g = one(og, source(graw, 3), p_diag)

    def inner_go(*copies_out):
        @pl.when(inner)
        def _():
            for c in copies_out:
                c.start()

    def wait_diag(direct, passed):
        @pl.when(inner)
        def _():
            direct.wait_recv()

        @pl.when(outer)
        def _():
            passed.wait_recv()

    def columns(ref, at, n):
        return ref.at[:, pl.ds(at, n)]

    def lines(ref, at, n):
        return ref.at[pl.ds(at, n)]

    c_wia = one(win.at[0, :, pl.ds(0, HA)], columns(wi, RA, HA), p_wgt)
    c_woa = one(wout.at[0, pl.ds(0, HA)], lines(wo, RA, HA), p_wgt)
    c_wib = one(win.at[0, :, pl.ds(HA, HB)], columns(wi, RB, HB), p_wgt)
    c_wob = one(wout.at[0, pl.ds(HA, HB)], lines(wo, RB, HB), p_wgt)
    c_wis = one(win.at[0], columns(wi, SIB, H), p_core)
    c_wos = one(wout.at[0], lines(wo, SIB, H), p_core)
    f_wia = one(columns(wi, RA, HA), columns(wi, RAS, HA), p_core)
    f_woa = one(lines(wo, RA, HA), lines(wo, RAS, HA), p_core)
    f_wib = one(columns(wi, RB, HB), columns(wi, RBS, HB), p_core)
    f_wob = one(lines(wo, RB, HB), lines(wo, RBS, HB), p_core)
    for c in [c_info[1], c_x[1], c_info[0], c_x[0], c_g[1], c_g[0]]:
        go(c)
    inner_go(d_info, d_x, d_g)
    go(c_wia)

    def codes(s):
        shift = (s % 2) * CAP - 1024.0 * z_lo.astype(f32)
        return info[s, 0:2, :] + shift

    def build(s):
        code = codes(s)
        g, at = s // 2, s % 2
        row = lax.broadcasted_iota(jnp.int32, (G, T), 0).astype(f32)
        hit = jnp.logical_or(row == code[0:1, :], row == code[1:2, :])
        pk[g * G : (g + 1) * G, at * T : (at + 1) * T] = jnp.where(hit, 1.0, 0.0).astype(bf16)
        lane = lax.broadcasted_iota(jnp.int32, (T, G), 1).astype(f32)
        hit = jnp.logical_or(lane == to_col(code[0:1, :]), lane == to_col(code[1:2, :]))
        pt[s * T : (s + 1) * T, :] = jnp.where(hit, 1.0, 0.0).astype(bf16)

    tile = G // 2

    def pack_x(g):
        raw = xraw[g * 2 * T : (g + 1) * 2 * T, :]
        for i in range(2):
            at = g * G + i * tile
            put_rows(xpk, g * Q + i * Q // 2, Q // 2, dot(pk[at : at + tile, :], raw))

    def pack_g(g):
        raw = graw[g * 2 * T : (g + 1) * 2 * T, :]
        for i in range(2):
            at = g * G + i * tile
            row = (lax.broadcasted_iota(jnp.int32, (tile, T), 0) + i * tile).astype(f32)
            gate = jnp.zeros((tile, T), f32)
            for s in (2 * g, 2 * g + 1):
                code = codes(s)
                for k in range(2):
                    gate += jnp.where(row == code[k : k + 1, :], info[s, 2 + k : 3 + k, :], 0.0)
            gate = jnp.sum(gate, axis=1, keepdims=True)
            put_rows(gpk, g * Q + i * Q // 2, Q // 2, dot(pk[at : at + tile, :], raw) * gate)

    build(0)
    for c in copies[:2]:
        c.wait()
    c_info[0].wait_recv()
    build(1)
    c_x[0].wait_recv()
    pack_x(0)
    send_all(xpk, xrv, sx, rx, 0, 6)
    c_info[1].wait_recv()
    inner_go(f_info)
    c_x[1].wait_recv()
    inner_go(f_x)
    for c in (c_woa, c_wis, c_wos):
        go(c)
    build(2)
    c_g[0].wait_recv()
    pack_g(0)
    send_all(gpk, grv, sg, rgs, 0, 8)
    c_g[1].wait_recv()
    inner_go(f_g)
    for c in (c_wib, c_wob):
        go(c)
    wait_diag(d_info, f_info)
    build(3)
    wait_diag(d_x, f_x)
    pack_x(1)
    send_all(xpk, xrv, sx, rx, 1, 6)
    wait_diag(d_g, f_g)
    pack_g(1)
    send_all(gpk, grv, sg, rgs, 1, 8)

    def slopes(at, n):
        @pl.loop(0, 2)
        def _(g):
            rows = pl.ds(pl.multiple_of(g * G, G), G)
            sl[rows, at : at + n] = gelu_slope(dot(rows_of(xrv, g * Q, Q), wi[:, at : at + n]))

    def grads(at, n, g):
        rows = slice(g * G, (g + 1) * G)
        act = dot_t(rows_of(grv, g * Q, Q), wo[at : at + n, :])
        pg[rows, at : at + n] = (act * sl[rows, at : at + n]).astype(bf16)

    copies[2].wait()
    c_wis.wait_recv()
    for g in range(2):
        wait_all(xpk, xrv, sx, rx, g, 6)
    slopes(OWN, 2 * H)
    xt[...] = rows_of(xrv, 0, 2 * Q).T
    c_wia.wait_recv()
    go(f_wia)
    f_wia.wait_recv()
    slopes(RA, 2 * HA)
    copies[3].wait()
    c_wos.wait_recv()
    wait_all(gpk, grv, sg, rgs, 0, 8)
    grads(OWN, 2 * H, 0)
    c_woa.wait_recv()
    go(f_woa)
    c_wib.wait_recv()
    go(f_wib)
    f_woa.wait_recv()
    grads(RA, 2 * HA, 0)
    f_wib.wait_recv()
    slopes(RB, 2 * HB)
    wait_all(gpk, grv, sg, rgs, 1, 8)
    grads(RA, 2 * HA, 1)

    c_ga = one(wsa, wra, p_core)
    c_gb = one(wsb, wrb, p_core)
    c_gc = one(wsc, wrc, p_core)
    c_za = one(za, zra, p_wgt)
    c_zb = one(zb, zrb, p_wgt)

    def partial_grad(at, n, kept, sent):
        @pl.loop(0, D // H)
        def _(i):
            rows = pl.ds(pl.multiple_of(i * H, H), H)
            part = dot(xt[rows, :], pg[:, at : at + 2 * n])
            kept[rows, :] = part[:, 0:n]
            sent[rows, :] = part[:, n : 2 * n].astype(bf16)

    partial_grad(RA, HA, wgr.at[:, 0:HA], wsa)
    go(c_ga)
    c_wob.wait_recv()
    go(f_wob)
    grads(OWN, 2 * H, 1)
    c_ga.wait_recv()
    za[...] = (wgr[:, 0:HA] + wra[...].astype(f32)).astype(bf16)
    go(c_za)
    f_wob.wait_recv()
    grads(RB, 2 * HB, 1)
    grads(RB, 2 * HB, 0)

    for g in (1, 0):
        put_rows(rg, g * Q, Q, dot_t(pg[g * G : (g + 1) * G, :], wi[...]))
        send_all(rg, rt, st, rts, g, 10)
    partial_grad(RB, HB, wgr.at[:, HA:H], wsb)
    go(c_gb)
    partial_grad(OWN, H, wg, wsc)
    go(c_gc)
    c_gb.wait_recv()
    zb[...] = (wgr[:, HA:H] + wrb[...].astype(f32)).astype(bf16)
    go(c_zb)
    c_gc.wait_recv()
    for c in copies[4:]:
        c.wait()

    def adam(at, n, arrived):
        cols = slice(at, at + n)
        grad = wg[:, cols] + wrc[:, cols].astype(f32) + arrived[...].astype(f32)
        first = beta_one * mm1[:, cols] + (1.0 - beta_one) * grad
        second = beta_two * mm2[:, cols] + (1.0 - beta_two) * grad * grad
        step = (first / (1.0 - beta_one**ADAM_STEP)) / (
            jnp.sqrt(second / (1.0 - beta_two**ADAM_STEP)) + adam_eps
        )
        an[:, cols] = step.astype(bf16)

    c_swa = one(columns(an, 0, HA), columns(ar, 0, HA), p_zlo)
    c_swb = one(columns(an, HA, HB), columns(ar, HA, HB), p_zlo)
    c_z1 = one(zs.at[pl.ds(T, T)], zr.at[pl.ds(T, T)], p_zlo)
    c_zd = one(zs.at[pl.ds(T, T)], zd, p_diag)
    c_z0 = one(zs.at[pl.ds(0, T)], zr.at[pl.ds(0, T)], p_zlo)
    c_back = one(xs, xr, p_row)
    outs = [
        local(12, columns(an, 0, HA), columns(ao, 0, HA)),
        local(13, columns(an, HA, HB), columns(ao, HA, HB)),
        local(14, keep.at[pl.ds(0, T)], xp),
    ]

    def combine(s):
        return dot(pt[s * T : (s + 1) * T, :], rows_of(rt, (s // 2) * Q, Q))

    wait_all(rg, rt, st, rts, 1, 10)
    zs[T : 2 * T, :] = combine(3).astype(bf16)

    @pl.when(inner)
    def _():
        c_zd.start()

    @pl.when(outer)
    def _():
        c_z1.start()

    keep[T : 2 * T, :] = combine(2)

    @pl.when(outer)
    def _():
        xs[...] = keep[T : 2 * T, :].astype(bf16)
        c_back.start()

    wait_all(rg, rt, st, rts, 0, 10)
    zs[0:T, :] = combine(1).astype(bf16)
    go(c_z0)
    keep[0:T, :] = combine(0)

    @pl.when(inner)
    def _():
        c_z1.wait_recv()
        xs[...] = (keep[T : 2 * T, :] + zr[T : 2 * T, :].astype(f32)).astype(bf16)
        c_back.start()

    c_za.wait_recv()
    adam(0, HA, zra)
    c_swa.start()
    outs[0].start()

    c_zb.wait_recv()
    adam(HA, HB, zrb)
    c_swb.start()
    outs[1].start()
    c_z0.wait_recv()
    keep[0:T, :] += zr[0:T, :].astype(f32)

    @pl.when(inner)
    def _():
        c_zd.wait_recv()
        keep[0:T, :] += zd[...].astype(f32)

    outs[2].start()

    @pl.loop(1, Q)
    def _(d):
        for g in range(2):
            send(xpk, xrv, sx, rx, g, d).wait_send()
            send(gpk, grv, sg, rgs, g, d).wait_send()
            send(rg, rt, st, rts, g, d).wait_send()

    for c in started:
        c.wait_send()

    @pl.when(inner)
    def _():
        for c in (d_info, d_x, d_g, f_info, f_x, f_g, c_zd):
            c.wait_send()

    @pl.when(outer)
    def _():
        c_z1.wait_send()

    for c in (c_swa, c_back, c_swb, *outs):
        c.wait()


def finish(swp, xp, xr, an, ar, xo, ao):
    e = lax.axis_index("expert")
    expert = lax.broadcasted_iota(jnp.int32, (1, E), 1)
    new_home = jnp.sum(jnp.where(expert == e, swp[...].astype(f32), 0.0), axis=1, keepdims=True)
    moved = jnp.broadcast_to(new_home != e.astype(f32), (ao.shape[0], T))
    for i in range(0, H, T):
        ao[:, i : i + T] = jnp.where(moved, ar[:, i : i + T], an[:, i : i + T])
    xo[...] = (xp[...] + xr[...].astype(f32)).astype(bf16)


def shards(tokens, out_grad, gates, expert_ids, swap_list, w_in, w_out, first_moment, second_moment):
    any_spec = pl.BlockSpec(memory_space=pl.ANY)
    vmem = pl.BlockSpec(memory_space=pltpu.VMEM)
    dma = pltpu.SemaphoreType.DMA
    xp, xr, an, ar = pl.pallas_call(
        kernel,
        out_shape=(
            jax.ShapeDtypeStruct((T, D), f32),
            jax.ShapeDtypeStruct((T, D), bf16),
            jax.ShapeDtypeStruct((D, H), bf16),
            jax.ShapeDtypeStruct((D, H), bf16),
        ),
        in_specs=[any_spec, any_spec, vmem, vmem, any_spec, any_spec, any_spec, any_spec],
        out_specs=(any_spec, any_spec, any_spec, any_spec),
        scratch_shapes=[
            pltpu.VMEM((4, 8, T), f32),
            pltpu.VMEM((4 * T, D), bf16),
            pltpu.VMEM((4 * T, D), bf16),
            pltpu.VMEM((R, 2 * T), bf16),
            pltpu.VMEM((4 * T, G), bf16),
            pltpu.VMEM((2 * Q, B, D), bf16),
            pltpu.VMEM((2 * Q, B, D), bf16),
            pltpu.VMEM((2 * Q, B, D), bf16),
            pltpu.VMEM((2 * Q, B, D), bf16),
            pltpu.VMEM((D, R), bf16),
            pltpu.VMEM((R, 4 * H), f32),
            pltpu.VMEM((D, 4 * H), bf16),
            pltpu.VMEM((4 * H, D), bf16),
            pltpu.VMEM((R, 4 * H), bf16),
            pltpu.VMEM((2 * Q, B, D), bf16),
            pltpu.VMEM((2 * Q, B, D), bf16),
            pltpu.VMEM((D, H), f32),
            pltpu.VMEM((D, H), f32),
            pltpu.VMEM((D, HA), bf16),
            pltpu.VMEM((D, HA), bf16),
            pltpu.VMEM((D, HB), bf16),
            pltpu.VMEM((D, HB), bf16),
            pltpu.VMEM((D, H), bf16),
            pltpu.VMEM((D, H), bf16),
            pltpu.VMEM((D, HA), bf16),
            pltpu.VMEM((D, HA), bf16),
            pltpu.VMEM((D, HB), bf16),
            pltpu.VMEM((D, HB), bf16),
            pltpu.VMEM((D, H), f32),
            pltpu.VMEM((D, H), f32),
            pltpu.VMEM((2 * T, D), bf16),
            pltpu.VMEM((2 * T, D), bf16),
            pltpu.VMEM((T, D), bf16),
            pltpu.VMEM((T, D), bf16),
            pltpu.VMEM((2 * T, D), f32),
            pltpu.VMEM((D, H), bf16),
            dma((N_ONE,)), dma((N_ONE,)), dma((N_LOCAL,)),
            dma((E,)), dma((E,)), dma((E,)), dma((E,)), dma((E,)), dma((E,)),
        ],
        compiler_params=pltpu.CompilerParams(
            collective_id=0, has_side_effects=True, vmem_limit_bytes=60 << 20
        ),
        name="experts",
    )(tokens, out_grad, expert_ids.T, gates.T, w_in, w_out, first_moment, second_moment)
    steps = 2
    rows = pl.BlockSpec((T // steps, D), lambda i: (i, 0))
    block = pl.BlockSpec((D // steps, H), lambda i: (i, 0))
    x_grad, adam_out = pl.pallas_call(
        finish,
        grid=(steps,),
        out_shape=(jax.ShapeDtypeStruct((T, D), bf16), jax.ShapeDtypeStruct((D, H), bf16)),
        in_specs=[pl.BlockSpec((1, E), lambda i: (0, 0)), rows, rows, block, block],
        out_specs=(rows, block),
        name="finish",
    )(swap_list[None], xp, xr, an, ar)
    return x_grad, adam_out[None]


def solution(mesh):
    token_spec = P(("dp", "expert"), None)
    in_specs = (
        token_spec, token_spec, token_spec, token_spec, P(),
        P("expert", None, "dp"), P("expert", "dp", None), P("expert", None, "dp"), P("expert", None, "dp"),
    )
    out_specs = (token_spec, P("expert", None, "dp"))
    return jax.shard_map(shards, mesh=mesh, in_specs=in_specs, out_specs=out_specs, check_vma=False)
```
